512 devices in a mesh: dp: 32 (over x, z), tensor: 16 (over y, core).
Axes of the slice: x: 4, y: 8, z: 8, core: 2. Of those that a mesh axis runs over, the one named last changes fastest.
Arguments:
- activations: bfloat16 [16384, 16384], P('dp', 'tensor'), may hold values from -40 to 40, as said below
- token_ids: int32 [16384], P('dp'), may hold values from 0 to 128004, as said below
- weight: bfloat16 [16384, 16384], P('dp', 'tensor'), may hold values from -6 to 6
- inv_chol: float32 [128, 128, 1024], P('tensor', 'dp'), may hold values from -1 to 2, as said below
- bit_widths: int32 [128], P('tensor'), may hold values from 2 to 8, as said below
Outputs:
- quantized: bfloat16 [16384, 16384], P('dp', 'tensor')
- gram_blocks: float32 [128, 128, 128], P('tensor', 'dp')
- block_errors: float32 [128, 4], replicated
The draws below stay inside these ranges and needn't reach their ends.
Inputs may be any that keep to these rules, and one draw needn't show every extreme that they name: `token_ids`: id 128004 marks padding. In the d-th aligned block of 512 tokens (d = 0 .. 31), exactly 170 + d*342//31 tokens are not padding, at positions drawn from the seed; the last block has no padding. `bit_widths`: each entry is 2, 3, 4 or 8. `inv_chol`: row i of block b, with j = b mod (8), holds a positive entry at column j*128+i, arbitrary entries at columns from (j+1)*128 on, and zeros elsewhere. `activations`: finite values.
All inputs are finite; a program needn't handle non-finite values.
Results may differ from the reference program's by a relative error of at most 0.001.
Values sent between devices are 32-bit elements; how exact they have to be, the bound alone decides.
No kernel may reach another device: no remote copies, remote signals or barrier semaphores. Data moves between devices by JAX's collectives and lax.ppermute only.
A program may use at most 64 MiB of HBM per device.

```python
import math
import jax
import jax.numpy as jnp
from jax import lax

D = 16384
OUT = 16384
BLK = 128
PANEL = 1024
TOK_DEV = 512
TOKENS = 16384
BLOCKS = 128


def draw_activations(key, part):
    first_key, second_key, third_key = jax.random.split(key, 3)
    row_scale = jnp.exp(jax.random.uniform(second_key, (TOKENS, 1), jnp.float32, math.log(0.3), math.log(3.0)))
    column_scale = jnp.exp(jax.random.uniform(third_key, (1, D), jnp.float32, math.log(0.5), math.log(2.0)))
    normal_part = jax.random.normal(first_key, (TOKENS, D), jnp.float32)
    return jnp.clip(normal_part * row_scale * column_scale, -40.0, 40.0).astype(jnp.bfloat16)


def draw_token_ids(key, part):
    block_count = TOKENS // TOK_DEV
    first_key, second_key = jax.random.split(key)
    fewest_live = TOK_DEV // 3
    live_counts = fewest_live + jnp.arange(block_count, dtype=jnp.int32) * (TOK_DEV - fewest_live) // max(block_count - 1, 1)
    block_keys = jax.random.split(second_key, block_count)
    position_rank = jax.vmap(lambda one_key: jax.random.permutation(one_key, TOK_DEV))(block_keys)
    word_ids = jax.random.randint(first_key, (block_count, TOK_DEV), 0, 128000)
    chosen = jnp.where(position_rank < live_counts[:, None], word_ids, 128004)
    return chosen.reshape(TOKENS).astype(jnp.int32)


def draw_inv_chol(key, part):
    per_panel = PANEL // BLK
    first_key, second_key = jax.random.split(key)
    block_index = jnp.arange(BLOCKS)[:, None, None] % per_panel
    row_index = jnp.arange(BLK)[None, :, None]
    column = jnp.arange(PANEL)[None, None, :]
    on_diagonal = column == block_index * BLK + row_index
    beyond = column >= (block_index + 1) * BLK
    diagonal_values = jnp.exp(jax.random.uniform(first_key, (BLOCKS, BLK, PANEL), jnp.float32, math.log(0.5), math.log(2.0)))
    spread = jnp.clip(jax.random.normal(second_key, (BLOCKS, BLK, PANEL), jnp.float32), -4.0, 4.0) * (0.5 / math.sqrt(PANEL))
    return jnp.where(on_diagonal, diagonal_values, jnp.where(beyond, spread, 0.0)).astype(jnp.float32)


def draw_bit_widths(key, part):
    width_index = jax.random.randint(key, (BLOCKS,), 0, 4)
    return jnp.where(width_index == 0, 2, jnp.where(width_index == 1, 3, jnp.where(width_index == 2, 4, 8))).astype(jnp.int32)


def block_levels(rng, dims, shards, smallest, high):
    loudness = 1.0
    for dim, parts in shards:
        steps = jax.random.uniform(jax.random.fold_in(jax.random.fold_in(rng, 6), dim), (parts,), jnp.float32, smallest / len(shards), high / len(shards))
        loudness = loudness * jnp.repeat(jnp.exp(steps), dims[dim] // parts).reshape((-1,) + (1,) * (len(dims) - 1 - dim))
    return loudness


def noise(rng, extent, width, reach, shards=(), kind=jnp.bfloat16):
    entries = jax.random.normal(rng, extent, jnp.float32) * width
    if len(shards) > 0:
        entries = block_levels(rng, extent, shards, -0.22, 0.18) * entries
    return jnp.clip(entries, min=-reach, max=reach).astype(kind)


def setup_inputs(seed: int = 0) -> dict:
    splits = jax.random.split(jax.random.key(seed), 6)
    activations = draw_activations(jax.random.fold_in(splits[5], 71), 0)
    token_ids = draw_token_ids(jax.random.fold_in(splits[5], 71), 0)
    weight = noise(splits[2], (OUT, D), 1.0, 6.0, ((0, 32), (1, 16)))
    inv_chol = draw_inv_chol(jax.random.fold_in(splits[5], 71), 0)
    bit_widths = draw_bit_widths(jax.random.fold_in(splits[5], 71), 0)
    return {"activations": activations, "token_ids": token_ids, "weight": weight, "inv_chol": inv_chol, "bit_widths": bit_widths}


pad_token = 128004


def level_count(widths):
    return jnp.where(widths == 2, 2.0, jnp.where(widths == 3, 4.0, jnp.where(widths == 4, 8.0, 128.0))).astype(jnp.float32)


def soft_quantize(values, levels):
    largest = jnp.max(jnp.abs(values), axis=-1, keepdims=True)
    step_size = (largest + 1e-6) / (levels - 0.5)
    scaled = values / step_size
    smooth = scaled - jnp.sin(2.0 * jnp.pi * scaled) / (2.0 * jnp.pi)
    return step_size * jnp.clip(smooth, -levels, levels - 1.0)


def reference(activations, token_ids, weight, inv_chol, bit_widths):
    live = (token_ids != pad_token).astype(jnp.float32)
    count = jnp.sum(live)
    stacked = activations.reshape(TOKENS, BLOCKS, BLK).transpose(1, 0, 2)
    live_rows = live.astype(activations.dtype)[:, None]

    def block_gram(block_piece):
        return jnp.dot((block_piece * live_rows).T, block_piece, preferred_element_type=jnp.float32)

    gram_blocks = lax.map(block_gram, stacked) / count

    weight_blocks = weight.reshape(OUT, BLOCKS, BLK).transpose(1, 0, 2)
    level_table = [2.0, 4.0, 8.0, 128.0]

    def block_error(operands):
        block_piece, gram = operands
        values = block_piece.astype(jnp.float32)
        results = []
        for width_slot in range(4):
            levels = level_table[width_slot]
            delta = values - soft_quantize(values, levels)
            weighted = jnp.dot(delta, gram, precision=lax.Precision.HIGHEST)
            results.append(jnp.sum(weighted * delta) * (levels * levels / (OUT * BLK)))
        return jnp.stack(results)

    block_errors = lax.map(block_error, (weight_blocks, gram_blocks))

    per_panel = PANEL // BLK
    panels = D // PANEL
    weight_panels = weight.reshape(OUT, panels, PANEL).transpose(1, 0, 2)
    factor_panels = inv_chol.reshape(panels, per_panel, BLK, PANEL)
    level_panels = level_count(bit_widths).reshape(panels, per_panel)

    def panel_quant(operands):
        panel_weight, factor, levels = operands
        current = panel_weight.astype(jnp.float32)
        outputs = []
        for column_block in range(per_panel):
            first_column = column_block * BLK
            block_values = current[:, first_column:first_column + BLK]
            quantized_block = soft_quantize(block_values, levels[column_block])
            outputs.append(quantized_block.astype(jnp.bfloat16))
            if column_block + 1 < per_panel:
                factor_rows = factor[column_block]
                diagonal = jnp.diagonal(factor_rows[:, first_column:first_column + BLK])
                scaled_error = (block_values - quantized_block) / diagonal[None, :]
                update = jnp.dot(scaled_error, factor_rows[:, first_column + BLK:], precision=lax.Precision.HIGHEST)
                current = jnp.concatenate([current[:, :first_column + BLK], current[:, first_column + BLK:] - update], axis=1)
        return jnp.concatenate(outputs, axis=1)

    quantized = lax.map(panel_quant, (weight_panels, factor_panels, level_panels))
    quantized = quantized.transpose(1, 0, 2).reshape(OUT, D)
    return quantized, gram_blocks, block_errors
```

```python
import jax
import jax.numpy as jnp
from jax import lax
from jax.experimental import pallas as pl
from jax.experimental.pallas import tpu as pltpu
from jax.sharding import Mesh, PartitionSpec as P

OUT = 16384
BLK = 128
PANEL = 1024
NB = 8
DP = 32
ROWS = BLK // DP
NX, NZ, NY, NC = 4, 8, 8, 2
PAIRS = [(j, c) for j in range(NB) for c in range(j + 1, NB)]
NP = len(PAIRS) + 1
PAD = 128004
LEVELS = (2.0, 4.0, 8.0, 128.0)

SIN = (
    0.9999996039231652,
    -6.579691570100355,
    12.986436001995736,
    -12.188101551479916,
    6.558042314696102,
    -1.9530321174789678,
)


def sine_over_two_pi(u):
    r = u - jnp.round(u)
    z = r * r
    p = SIN[-1] * z + SIN[-2]
    for a in SIN[-3::-1]:
        p = p * z + a
    return p * r


def params(*semantics):
    return pltpu.CompilerParams(dimension_semantics=semantics, vmem_limit_bytes=56 << 20)


def pack_kernel(first_ref, f_ref, o_ref):
    lane = lax.broadcasted_iota(jnp.int32, (ROWS, BLK), 1)
    row = lax.broadcasted_iota(jnp.int32, (ROWS, BLK), 0)
    on_diag = lane == row + first_ref[0]
    diag = jnp.zeros((ROWS, BLK), jnp.float32)
    for j in range(NB):
        tile = f_ref[j, :, j * BLK : (j + 1) * BLK]
        value = jnp.sum(jnp.where(on_diag, tile, 0.0), axis=1, keepdims=True)
        diag = jnp.where(lane == j, value, diag)
    for i in range(NZ):
        for p, (j, c) in enumerate(PAIRS):
            o_ref[i, p] = f_ref[j, :, c * BLK : (c + 1) * BLK]
        o_ref[i, NP - 1] = diag


def pack_factor(first, factor):
    return pl.pallas_call(
        pack_kernel,
        out_shape=jax.ShapeDtypeStruct((NZ, NP, ROWS, BLK), jnp.float32),
        in_specs=[
            pl.BlockSpec(memory_space=pltpu.SMEM),
            pl.BlockSpec(memory_space=pltpu.VMEM),
        ],
        out_specs=pl.BlockSpec(memory_space=pltpu.VMEM),
        compiler_params=params(),
        name="pack_factor",
    )(first, factor)


def gram_kernel(tok_ref, a_ref, o_ref):
    live = jnp.where(tok_ref[...] != PAD, 1.0, 0.0).astype(jnp.bfloat16)
    x = a_ref[...]
    g = jnp.dot(x.T * live, x, preferred_element_type=jnp.float32)
    for d in range(DP):
        o_ref[d, 0] = g[d * ROWS : (d + 1) * ROWS]


def gram_partial(tokens, activations):
    n = activations.shape[0]
    return pl.pallas_call(
        gram_kernel,
        out_shape=jax.ShapeDtypeStruct((DP, NB, ROWS, BLK), jnp.float32),
        grid=(NB,),
        in_specs=[
            pl.BlockSpec((1, n), lambda b: (0, 0)),
            pl.BlockSpec((n, BLK), lambda b: (0, b)),
        ],
        out_specs=pl.BlockSpec((DP, 1, ROWS, BLK), lambda b: (0, b, 0, 0)),
        compiler_params=params("arbitrary"),
        name="gram_partial",
    )(tokens, activations)


def sum_kernel(g_ref, own_ref, o_ref):
    total = g_ref[0]
    for d in range(1, DP):
        total = total + g_ref[d]
    own_ref[...] = total
    for d in range(DP):
        o_ref[d] = total


def sum_rows(received):
    return pl.pallas_call(
        sum_kernel,
        out_shape=(
            jax.ShapeDtypeStruct((NB, ROWS, BLK), jnp.float32),
            jax.ShapeDtypeStruct((DP, NB, ROWS, BLK), jnp.float32),
        ),
        in_specs=[pl.BlockSpec(memory_space=pltpu.VMEM)],
        out_specs=(pl.BlockSpec(memory_space=pltpu.VMEM),) * 2,
        compiler_params=params(),
        name="sum_rows",
    )(received)


def error_kernel(w_ref, o_ref):
    w = w_ref[...].astype(jnp.float32)
    bound = jnp.max(jnp.abs(w), axis=1, keepdims=True) + 1e-6
    unit = w * (1.0 / bound)
    for k, levels in enumerate(LEVELS):
        u = unit * (levels - 0.5)
        smooth = jnp.clip(u - sine_over_two_pi(u), -levels, levels - 1.0)
        e = (w - (bound * (1.0 / (levels - 0.5))) * smooth).astype(jnp.bfloat16)
        s = lax.dot_general(e, e, (((0,), (0,)), ((), ())), preferred_element_type=jnp.float32)
        for d in range(DP):
            o_ref[0, k, d] = s[d * ROWS : (d + 1) * ROWS]


def error_grams(weight):
    rows = weight.shape[0]
    return pl.pallas_call(
        error_kernel,
        out_shape=jax.ShapeDtypeStruct((NB, 4, DP, ROWS, BLK), jnp.float32),
        grid=(NB,),
        in_specs=[pl.BlockSpec((rows, BLK), lambda b: (0, b))],
        out_specs=pl.BlockSpec((1, 4, DP, ROWS, BLK), lambda b: (b, 0, 0, 0, 0)),
        compiler_params=params("arbitrary"),
        name="error_grams",
    )(weight)


def score_kernel(tok_ref, g_ref, s_ref, o_ref):
    b = pl.program_id(0)
    lane = lax.broadcasted_iota(jnp.int32, (1, BLK), 1)

    @pl.when(b == 0)
    def _():
        live = jnp.sum(jnp.where(tok_ref[...] != PAD, 1.0, 0.0))
        o_ref[...] = jnp.where(lane == 4 * NB, live, 0.0)

    row = o_ref[...]
    for k in range(4):
        acc = g_ref[0, 0] * s_ref[0, k, 0]
        for d in range(1, DP):
            acc = acc + g_ref[d, 0] * s_ref[0, k, d]
        row = jnp.where(lane == 4 * b + k, jnp.sum(acc), row)
    o_ref[...] = row


def scores(tokens, gram, grams):
    n = tokens.shape[1]
    return pl.pallas_call(
        score_kernel,
        out_shape=jax.ShapeDtypeStruct((1, BLK), jnp.float32),
        grid=(NB,),
        in_specs=[
            pl.BlockSpec((1, n), lambda b: (0, 0)),
            pl.BlockSpec((DP, 1, ROWS, BLK), lambda b: (0, b, 0, 0)),
            pl.BlockSpec((1, 4, DP, ROWS, BLK), lambda b: (b, 0, 0, 0, 0)),
        ],
        out_specs=pl.BlockSpec((1, BLK), lambda b: (0, 0)),
        compiler_params=params("arbitrary"),
        name="scores",
    )(tokens, gram, grams)


CHUNKS = 2


def quant_kernel(bits_ref, x_ref, w_ref, own_ref, left_ref, right_ref, far0_ref, far1_ref, o_ref, c_ref, u_ref, slab_ref):
    rows = w_ref.shape[0] // CHUNKS
    x = x_ref[0]

    def slab(p):
        for off, refs in ((0, (own_ref,)), (NX - 1, (left_ref,)), (1, (right_ref,)), (2, (far0_ref, far1_ref))):
            base = pl.multiple_of(lax.rem(x + off, NX) * (NZ * ROWS), NZ * ROWS)
            chunk = jnp.concatenate([ref[i, p] for ref in refs for i in range(ref.shape[0])], axis=0)
            slab_ref[pl.ds(base, NZ * ROWS), :] = chunk
        return slab_ref[...]

    inv_diag = 1.0 / slab(NP - 1)[:, :NB].T
    p = 0
    for j in range(NB):
        first = j * BLK
        width = PANEL - first - BLK
        if width:
            for i in range(width // BLK):
                u = slab(p)
                p += 1
                high = u.astype(jnp.bfloat16)
                low = (u - high.astype(jnp.float32)).astype(jnp.bfloat16)
                cols = slice(i * BLK, (i + 1) * BLK)
                u_ref[0:BLK, cols] = high
                u_ref[BLK : 2 * BLK, cols] = high
                u_ref[2 * BLK : 3 * BLK, cols] = low
        bits = bits_ref[j]
        levels = jnp.where(bits == 2, 2.0, jnp.where(bits == 3, 4.0, jnp.where(bits == 4, 8.0, 128.0)))
        half = levels - 0.5
        for h in range(CHUNKS):
            part = slice(h * rows, (h + 1) * rows)
            if j == 0:
                c = w_ref[part, :BLK].astype(jnp.float32)
            else:
                c = c_ref[part, first : first + BLK]
            step = (jnp.max(jnp.abs(c), axis=1, keepdims=True) + 1e-6) / half
            u = c * (1.0 / step)
            q = step * jnp.clip(u - sine_over_two_pi(u), -levels, levels - 1.0)
            o_ref[part, first : first + BLK] = q.astype(jnp.bfloat16)
            if width:
                e = (c - q) * inv_diag[j : j + 1, :]
                high = e.astype(jnp.bfloat16)
                low = (e - high.astype(jnp.float32)).astype(jnp.bfloat16)
                lhs = jnp.concatenate([high, low, high], axis=1)
                update = jnp.dot(lhs, u_ref[:, :width], preferred_element_type=jnp.float32)
                if j == 0:
                    rest = w_ref[part, BLK:].astype(jnp.float32)
                else:
                    rest = c_ref[part, first + BLK :]
                c_ref[part, first + BLK :] = rest - update


def quantize(bits, x, weight, factor):
    rows = weight.shape[0]
    return pl.pallas_call(
        quant_kernel,
        out_shape=jax.ShapeDtypeStruct((rows, PANEL), jnp.bfloat16),
        in_specs=[
            pl.BlockSpec(memory_space=pltpu.SMEM),
            pl.BlockSpec(memory_space=pltpu.SMEM),
        ]
        + [pl.BlockSpec(memory_space=pltpu.VMEM)] * 6,
        out_specs=pl.BlockSpec(memory_space=pltpu.VMEM),
        scratch_shapes=[
            pltpu.VMEM((rows, PANEL), jnp.float32),
            pltpu.VMEM((3 * BLK, PANEL - BLK), jnp.bfloat16),
            pltpu.VMEM((BLK, BLK), jnp.float32),
        ],
        compiler_params=params(),
        name="quantize",
    )(bits, x, weight, *factor)


def exchange(pieces, axes):
    return lax.all_to_all(pieces, axes, 0, 0, tiled=False)


def to_all(piece, axes, count):
    return exchange(jnp.broadcast_to(piece[None], (count,) + piece.shape), axes)


def shift_x(piece, by):
    return lax.ppermute(piece, "x", [(i, (i + by) % NX) for i in range(NX)])


def per_device(activations, token_ids, weight, inv_chol, bit_widths):
    dp = ("x", "z")
    tensor = ("y", "c")
    half = NZ // 2
    tokens = token_ids.reshape(1, -1)
    x = lax.axis_index("x").reshape(1).astype(jnp.int32)
    first = (lax.axis_index(dp) * ROWS).reshape(1).astype(jnp.int32)
    packed = pack_factor(first, inv_chol)
    over_z = exchange(packed, "z")
    partial = gram_partial(tokens, activations)
    grams = error_grams(weight)
    over_z, partial = lax.optimization_barrier((over_z, partial))
    gram_rows = exchange(partial, dp)
    left = shift_x(over_z, 1)
    right = shift_x(over_z, -1)
    far0 = shift_x(left[:half], 1)
    far1 = shift_x(right[half:], -1)
    own, copies = sum_rows(gram_rows)
    gram = exchange(copies, dp)
    row = scores(tokens, gram, grams)
    row = to_all(row, dp, DP)
    row = jnp.sum(row, axis=0)
    rows = to_all(row, tensor, NY * NC)[:, 0]
    quantized = quantize(bit_widths, x, weight, (over_z, left, right, far0, far1))
    count = row[0, 4 * NB]
    scale = jnp.array([l * l / (OUT * BLK) for l in LEVELS], jnp.float32) / count
    block_errors = rows[:, : 4 * NB].reshape(-1, 4) * scale
    return quantized, own / count, block_errors


def solution(mesh):
    fine = Mesh(mesh.devices.reshape(NX, NZ, NY, NC), ("x", "z", "y", "c"))
    dp = ("x", "z")
    tensor = ("y", "c")
    placed = (P(dp, tensor), P(dp), P(dp, tensor), P(tensor, dp, None), P(tensor))
    return jax.shard_map(
        per_device,
        mesh=fine,
        in_specs=placed,
        out_specs=(P(dp, tensor), P(tensor, dp, None), P()),
        check_vma=False,
    )
```

```python
import jax
import jax.numpy as jnp
from jax import lax
from jax.experimental import pallas as pl
from jax.experimental.pallas import tpu as pltpu
from jax.sharding import Mesh, PartitionSpec as P

OUT = 16384
BLK = 128
PANEL = 1024
NB = 8
DP = 32
ROWS = BLK // DP
NX, NZ, NY, NC = 4, 8, 8, 2
PAIRS = [(j, c) for j in range(NB) for c in range(j + 1, NB)]
NP = len(PAIRS) + 1
PAD = 128004
LEVELS = (2.0, 4.0, 8.0, 128.0)

SIN = (
    0.9999996039231652,
    -6.579691570100355,
    12.986436001995736,
    -12.188101551479916,
    6.558042314696102,
    -1.9530321174789678,
)


def sine_over_two_pi(u):
    r = u - jnp.round(u)
    z = r * r
    p = SIN[-1] * z + SIN[-2]
    for a in SIN[-3::-1]:
        p = p * z + a
    return p * r


def params(*semantics):
    return pltpu.CompilerParams(dimension_semantics=semantics, vmem_limit_bytes=56 << 20)


def pack_kernel(first_ref, f_ref, tok_ref, a_ref, o_ref):
    lane = lax.broadcasted_iota(jnp.int32, (ROWS, BLK), 1)
    row = lax.broadcasted_iota(jnp.int32, (ROWS, BLK), 0)
    on_diag = lane == row + first_ref[0]
    diag = jnp.zeros((ROWS, BLK), jnp.float32)
    for j in range(NB):
        tile = f_ref[j, :, j * BLK : (j + 1) * BLK]
        value = jnp.sum(jnp.where(on_diag, tile, 0.0), axis=1, keepdims=True)
        diag = jnp.where(lane == j, value, diag)
    for i in range(NZ):
        o_ref[i, NP - 1] = diag
    for p, (j, c) in enumerate(PAIRS):
        tile = f_ref[j, :, c * BLK : (c + 1) * BLK]
        for i in range(NZ):
            o_ref[i, p] = tile
    live = jnp.where(tok_ref[...] != PAD, 1.0, 0.0).astype(jnp.bfloat16)
    for b in range(NB):
        x = a_ref[:, b * BLK : (b + 1) * BLK]
        g = jnp.dot(x.T * live, x, preferred_element_type=jnp.float32)
        for d in range(DP):
            o_ref[d % NZ, NP + (d // NZ) * NB + b] = g[d * ROWS : (d + 1) * ROWS]


def pack(first, factor, tokens, activations):
    vmem = pl.BlockSpec(memory_space=pltpu.VMEM)
    return pl.pallas_call(
        pack_kernel,
        out_shape=jax.ShapeDtypeStruct((NZ, NP + NX * NB, ROWS, BLK), jnp.float32),
        in_specs=[pl.BlockSpec(memory_space=pltpu.SMEM), vmem, vmem, vmem],
        out_specs=vmem,
        compiler_params=params(),
        name="pack",
    )(first, factor, tokens, activations)


def sum_z_kernel(g_ref, o_ref):
    for x in range(NX):
        tiles = slice(NP + x * NB, NP + (x + 1) * NB)
        total = g_ref[0, tiles]
        for i in range(1, NZ):
            total = total + g_ref[i, tiles]
        o_ref[x] = total


def sum_z(received):
    vmem = pl.BlockSpec(memory_space=pltpu.VMEM)
    return pl.pallas_call(
        sum_z_kernel,
        out_shape=jax.ShapeDtypeStruct((NX, NB, ROWS, BLK), jnp.float32),
        in_specs=[vmem],
        out_specs=vmem,
        compiler_params=params(),
        name="sum_z",
    )(received)


def sum_x_kernel(g_ref, own_ref, o_ref):
    total = g_ref[0]
    for x in range(1, NX):
        total = total + g_ref[x]
    own_ref[...] = total
    for d in range(DP):
        o_ref[d] = total


def sum_x(received):
    vmem = pl.BlockSpec(memory_space=pltpu.VMEM)
    return pl.pallas_call(
        sum_x_kernel,
        out_shape=(
            jax.ShapeDtypeStruct((NB, ROWS, BLK), jnp.float32),
            jax.ShapeDtypeStruct((DP, NB, ROWS, BLK), jnp.float32),
        ),
        in_specs=[vmem],
        out_specs=(vmem, vmem),
        compiler_params=params(),
        name="sum_x",
    )(received)


def error_kernel(w_ref, o_ref):
    w = w_ref[...].astype(jnp.float32)
    bound = jnp.max(jnp.abs(w), axis=1, keepdims=True) + 1e-6
    unit = w * (1.0 / bound)
    for k, levels in enumerate(LEVELS):
        u = unit * (levels - 0.5)
        smooth = jnp.clip(u - sine_over_two_pi(u), -levels, levels - 1.0)
        e = (w - (bound * (1.0 / (levels - 0.5))) * smooth).astype(jnp.bfloat16)
        s = lax.dot_general(e, e, (((0,), (0,)), ((), ())), preferred_element_type=jnp.float32)
        for d in range(DP):
            o_ref[0, k, d] = s[d * ROWS : (d + 1) * ROWS]


def error_grams(weight):
    rows = weight.shape[0]
    return pl.pallas_call(
        error_kernel,
        out_shape=jax.ShapeDtypeStruct((NB, 4, DP, ROWS, BLK), jnp.float32),
        grid=(NB,),
        in_specs=[pl.BlockSpec((rows, BLK), lambda b: (0, b))],
        out_specs=pl.BlockSpec((1, 4, DP, ROWS, BLK), lambda b: (b, 0, 0, 0, 0)),
        compiler_params=params("arbitrary"),
        name="error_grams",
    )(weight)


def score_kernel(tok_ref, g_ref, s_ref, o_ref, row_ref):
    row_ref[...] = jnp.zeros((BLK, BLK), jnp.float32)
    live = jnp.where(tok_ref[...] != PAD, 1.0, 0.0)
    row_ref[4 * NB : 4 * NB + 1, :] = sum(live[:, i : i + BLK] for i in range(0, live.shape[1], BLK))
    for b in range(NB):
        for k in range(4):
            acc = g_ref[0, b] * s_ref[b, k, 0]
            for d in range(1, DP):
                acc = acc + g_ref[d, b] * s_ref[b, k, d]
            row_ref[k * NB + b : k * NB + b + 1, :] = jnp.sum(acc, axis=0, keepdims=True)
    row = jnp.sum(row_ref[...].T, axis=0, keepdims=True)
    for d in range(DP):
        o_ref[d] = row


def scores(tokens, gram, grams):
    vmem = pl.BlockSpec(memory_space=pltpu.VMEM)
    return pl.pallas_call(
        score_kernel,
        out_shape=jax.ShapeDtypeStruct((DP, 1, BLK), jnp.float32),
        in_specs=[vmem] * 3,
        out_specs=vmem,
        scratch_shapes=[pltpu.VMEM((BLK, BLK), jnp.float32)],
        compiler_params=params(),
        name="scores",
    )(tokens, gram, grams)


def total_kernel(r_ref, own_ref, gram_ref, o_ref):
    row = r_ref[0]
    for d in range(1, DP):
        row = row + r_ref[d]
    lane = lax.broadcasted_iota(jnp.int32, (1, BLK), 1)
    count = jnp.sum(jnp.where(lane == 4 * NB, row, 0.0))
    gram_ref[...] = own_ref[...] / count
    scale = jnp.zeros((1, BLK), jnp.float32)
    for k, levels in enumerate(LEVELS):
        scale = jnp.where(lane // NB == k, levels * levels / (OUT * BLK), scale)
    row = row * scale / count
    for t in range(NY * NC):
        o_ref[t] = row


def totals(rows, own):
    vmem = pl.BlockSpec(memory_space=pltpu.VMEM)
    return pl.pallas_call(
        total_kernel,
        out_shape=(
            jax.ShapeDtypeStruct((NB, ROWS, BLK), jnp.float32),
            jax.ShapeDtypeStruct((NY * NC, 1, BLK), jnp.float32),
        ),
        in_specs=[vmem, vmem],
        out_specs=(vmem, vmem),
        compiler_params=params(),
        name="totals",
    )(rows, own)


def spread_kernel(r_ref, o_ref, row_ref):
    n = NY * NC
    for t in range(n):
        row_ref[t : t + 1, :] = r_ref[t]
    lane = lax.broadcasted_iota(jnp.int32, (8, BLK), 1)
    source = lax.broadcasted_iota(jnp.int32, (8, BLK), 0)
    total = [jnp.zeros((1, BLK), jnp.float32)] * 4
    for h in range(n // 8):
        skewed = pltpu.roll(row_ref[h * 8 : (h + 1) * 8, :], 0, 1, stride=NB, stride_axis=0)
        for k in range(4):
            moved = pltpu.roll(skewed, (h * 8 * NB - k * NB) % BLK, 1)
            kept = jnp.where(lane // NB == source + h * 8, moved, 0.0)
            total[k] = total[k] + jnp.sum(kept, axis=0, keepdims=True)
    for k in range(4):
        o_ref[k : k + 1, :] = total[k]


def spread(rows):
    vmem = pl.BlockSpec(memory_space=pltpu.VMEM)
    return pl.pallas_call(
        spread_kernel,
        out_shape=jax.ShapeDtypeStruct((4, BLK), jnp.float32),
        in_specs=[vmem],
        out_specs=vmem,
        scratch_shapes=[pltpu.VMEM((NY * NC, BLK), jnp.float32)],
        compiler_params=params(),
        name="spread",
    )(rows)


CHUNKS = 2


def quant_kernel(bits_ref, x_ref, w_ref, own_ref, left_ref, right_ref, far_ref, o_ref, c_ref, u_ref, slab_ref):
    rows = w_ref.shape[0] // CHUNKS
    x = x_ref[0]

    def slab(p):
        for off, ref in enumerate((own_ref, right_ref, far_ref, left_ref)):
            base = pl.multiple_of(lax.rem(x + off, NX) * (NZ * ROWS), NZ * ROWS)
            chunk = jnp.concatenate([ref[i, p] for i in range(NZ)], axis=0)
            slab_ref[pl.ds(base, NZ * ROWS), :] = chunk
        return slab_ref[...]

    inv_diag = 1.0 / slab(NP - 1)[:, :NB].T
    p = 0
    for j in range(NB):
        first = j * BLK
        width = PANEL - first - BLK
        if width:
            for i in range(width // BLK):
                u = slab(p)
                p += 1
                high = u.astype(jnp.bfloat16)
                low = (u - high.astype(jnp.float32)).astype(jnp.bfloat16)
                cols = slice(i * BLK, (i + 1) * BLK)
                u_ref[0:BLK, cols] = high
                u_ref[BLK : 2 * BLK, cols] = high
                u_ref[2 * BLK : 3 * BLK, cols] = low
        bits = bits_ref[j]
        levels = jnp.where(bits == 2, 2.0, jnp.where(bits == 3, 4.0, jnp.where(bits == 4, 8.0, 128.0)))
        half = levels - 0.5
        for h in range(CHUNKS):
            part = slice(h * rows, (h + 1) * rows)
            if j == 0:
                c = w_ref[part, :BLK].astype(jnp.float32)
            else:
                c = c_ref[part, first : first + BLK]
            step = (jnp.max(jnp.abs(c), axis=1, keepdims=True) + 1e-6) / half
            u = c * (1.0 / step)
            q = step * jnp.clip(u - sine_over_two_pi(u), -levels, levels - 1.0)
            o_ref[part, first : first + BLK] = q.astype(jnp.bfloat16)
            if width:
                e = (c - q) * inv_diag[j : j + 1, :]
                high = e.astype(jnp.bfloat16)
                low = (e - high.astype(jnp.float32)).astype(jnp.bfloat16)
                lhs = jnp.concatenate([high, low, high], axis=1)
                update = jnp.dot(lhs, u_ref[:, :width], preferred_element_type=jnp.float32)
                if j == 0:
                    rest = w_ref[part, BLK:].astype(jnp.float32)
                else:
                    rest = c_ref[part, first + BLK :]
                c_ref[part, first + BLK :] = rest - update


def quantize(bits, x, weight, factor):
    rows = weight.shape[0]
    return pl.pallas_call(
        quant_kernel,
        out_shape=jax.ShapeDtypeStruct((rows, PANEL), jnp.bfloat16),
        in_specs=[
            pl.BlockSpec(memory_space=pltpu.SMEM),
            pl.BlockSpec(memory_space=pltpu.SMEM),
        ]
        + [pl.BlockSpec(memory_space=pltpu.VMEM)] * 5,
        out_specs=pl.BlockSpec(memory_space=pltpu.VMEM),
        scratch_shapes=[
            pltpu.VMEM((rows, PANEL), jnp.float32),
            pltpu.VMEM((3 * BLK, PANEL - BLK), jnp.bfloat16),
            pltpu.VMEM((BLK, BLK), jnp.float32),
        ],
        compiler_params=params(),
        name="quantize",
    )(bits, x, weight, *factor)


def exchange(pieces, axes):
    return lax.all_to_all(pieces, axes, 0, 0, tiled=False)


def shift_x(piece, by):
    return lax.ppermute(piece, "x", [(i, (i + by) % NX) for i in range(NX)])


def per_device(activations, token_ids, weight, inv_chol, bit_widths):
    dp = ("x", "z")
    tensor = ("y", "c")
    tokens = token_ids.reshape(1, -1)
    x = lax.axis_index("x").reshape(1).astype(jnp.int32)
    first = (lax.axis_index(dp) * ROWS).reshape(1).astype(jnp.int32)
    packed = pack(first, inv_chol, tokens, activations)
    over_z = exchange(packed, "z")
    grams = error_grams(weight)
    rows = sum_z(over_z)
    rows = exchange(rows, "x")
    own, copies = sum_x(rows)
    gram = exchange(copies, dp)
    mine, _ = lax.optimization_barrier((over_z, copies))
    mine = mine[:, :NP]
    left = shift_x(mine, 1)
    right = shift_x(mine, -1)
    row = scores(tokens, gram, grams)
    left_late, _ = lax.optimization_barrier((left, row))
    row = exchange(row, dp)
    far = shift_x(left_late, 1)
    gram_out, row = totals(row, own)
    rows = exchange(row, tensor)
    quantized = quantize(bit_widths, x, weight, (mine, left, right, far))
    block_errors = spread(rows).T
    return quantized, gram_out, block_errors


def solution(mesh):
    fine = Mesh(mesh.devices.reshape(NX, NZ, NY, NC), ("x", "z", "y", "c"))
    dp = ("x", "z")
    tensor = ("y", "c")
    placed = (P(dp, tensor), P(dp), P(dp, tensor), P(tensor, dp, None), P(tensor))
    return jax.shard_map(
        per_device,
        mesh=fine,
        in_specs=placed,
        out_specs=(P(dp, tensor), P(tensor, dp, None), P()),
        check_vma=False,
    )
```

```python
import jax
import jax.numpy as jnp
from jax import lax
from jax.experimental import pallas as pl
from jax.experimental.pallas import tpu as pltpu
from jax.sharding import Mesh, PartitionSpec as P

OUT = 16384
BLK = 128
PANEL = 1024
NB = 8
DP = 32
ROWS = BLK // DP
NX, NZ, NY, NC = 4, 8, 8, 2
PAIRS = [(j, c) for j in range(NB) for c in range(j + 1, NB)]
NP = len(PAIRS) + 1
PAD = 128004
LEVELS = (2.0, 4.0, 8.0, 128.0)

SIN = (
    0.9999996039231652,
    -6.579691570100355,
    12.986436001995736,
    -12.188101551479916,
    6.558042314696102,
    -1.9530321174789678,
)


def sine_over_two_pi(u):
    r = u - jnp.round(u)
    z = r * r
    p = SIN[-1] * z + SIN[-2]
    for a in SIN[-3::-1]:
        p = p * z + a
    return p * r


def params(*semantics):
    return pltpu.CompilerParams(dimension_semantics=semantics, vmem_limit_bytes=56 << 20)


def gram_kernel(tok_ref, a_ref, o_ref):
    live = jnp.where(tok_ref[...] != PAD, 1.0, 0.0).astype(jnp.bfloat16)
    for b in range(NB):
        x = a_ref[:, b * BLK : (b + 1) * BLK]
        g = jnp.dot(x.T * live, x, preferred_element_type=jnp.float32)
        for d in range(DP):
            o_ref[d // NZ, d % NZ, b] = g[d * ROWS : (d + 1) * ROWS]


def gram_partial(tokens, activations):
    vmem = pl.BlockSpec(memory_space=pltpu.VMEM)
    return pl.pallas_call(
        gram_kernel,
        out_shape=jax.ShapeDtypeStruct((NX, NZ, NB, ROWS, BLK), jnp.float32),
        in_specs=[vmem, vmem],
        out_specs=vmem,
        compiler_params=params(),
        name="gram_partial",
    )(tokens, activations)


def sum_x_kernel(first_ref, f_ref, g_ref, o_ref):
    lane = lax.broadcasted_iota(jnp.int32, (ROWS, BLK), 1)
    row = lax.broadcasted_iota(jnp.int32, (ROWS, BLK), 0)
    on_diag = lane == row + first_ref[0]
    diag = jnp.zeros((ROWS, BLK), jnp.float32)
    for j in range(NB):
        tile = f_ref[j, :, j * BLK : (j + 1) * BLK]
        value = jnp.sum(jnp.where(on_diag, tile, 0.0), axis=1, keepdims=True)
        diag = jnp.where(lane == j, value, diag)
    for i in range(NZ):
        o_ref[i, NP - 1] = diag
    for p, (j, c) in enumerate(PAIRS):
        tile = f_ref[j, :, c * BLK : (c + 1) * BLK]
        for i in range(NZ):
            o_ref[i, p] = tile
    for i in range(NZ):
        total = g_ref[0, i]
        for x in range(1, NX):
            total = total + g_ref[x, i]
        o_ref[i, NP:] = total


def sum_x(first, factor, received):
    vmem = pl.BlockSpec(memory_space=pltpu.VMEM)
    return pl.pallas_call(
        sum_x_kernel,
        out_shape=jax.ShapeDtypeStruct((NZ, NP + NB, ROWS, BLK), jnp.float32),
        in_specs=[pl.BlockSpec(memory_space=pltpu.SMEM), vmem, vmem],
        out_specs=vmem,
        compiler_params=params(),
        name="sum_x",
    )(first, factor, received)


def sum_z_kernel(g_ref, own_ref, o_ref):
    total = g_ref[0, NP:]
    for i in range(1, NZ):
        total = total + g_ref[i, NP:]
    own_ref[...] = total
    for d in range(DP):
        o_ref[d] = total


def sum_z(received):
    vmem = pl.BlockSpec(memory_space=pltpu.VMEM)
    return pl.pallas_call(
        sum_z_kernel,
        out_shape=(
            jax.ShapeDtypeStruct((NB, ROWS, BLK), jnp.float32),
            jax.ShapeDtypeStruct((DP, NB, ROWS, BLK), jnp.float32),
        ),
        in_specs=[vmem],
        out_specs=(vmem, vmem),
        compiler_params=params(),
        name="sum_z",
    )(received)


def error_kernel(w_ref, o_ref):
    w = w_ref[...].astype(jnp.float32)
    bound = jnp.max(jnp.abs(w), axis=1, keepdims=True) + 1e-6
    unit = w * (1.0 / bound)
    for k, levels in enumerate(LEVELS):
        u = unit * (levels - 0.5)
        smooth = jnp.clip(u - sine_over_two_pi(u), -levels, levels - 1.0)
        e = (w - (bound * (1.0 / (levels - 0.5))) * smooth).astype(jnp.bfloat16)
        s = lax.dot_general(e, e, (((0,), (0,)), ((), ())), preferred_element_type=jnp.float32)
        for d in range(DP):
            o_ref[0, k, d] = s[d * ROWS : (d + 1) * ROWS]


def error_grams(weight):
    rows = weight.shape[0]
    return pl.pallas_call(
        error_kernel,
        out_shape=jax.ShapeDtypeStruct((NB, 4, DP, ROWS, BLK), jnp.float32),
        grid=(NB,),
        in_specs=[pl.BlockSpec((rows, BLK), lambda b: (0, b))],
        out_specs=pl.BlockSpec((1, 4, DP, ROWS, BLK), lambda b: (b, 0, 0, 0, 0)),
        compiler_params=params("arbitrary"),
        name="error_grams",
    )(weight)


def score_kernel(tok_ref, g_ref, s_ref, o_ref, row_ref):
    row_ref[...] = jnp.zeros((BLK, BLK), jnp.float32)
    live = jnp.where(tok_ref[...] != PAD, 1.0, 0.0)
    row_ref[4 * NB : 4 * NB + 1, :] = sum(live[:, i : i + BLK] for i in range(0, live.shape[1], BLK))
    for b in range(NB):
        for k in range(4):
            acc = g_ref[0, b] * s_ref[b, k, 0]
            for d in range(1, DP):
                acc = acc + g_ref[d, b] * s_ref[b, k, d]
            row_ref[k * NB + b : k * NB + b + 1, :] = jnp.sum(acc, axis=0, keepdims=True)
    row = jnp.sum(row_ref[...].T, axis=0, keepdims=True)
    for d in range(DP):
        o_ref[d] = row


def scores(tokens, gram, grams):
    vmem = pl.BlockSpec(memory_space=pltpu.VMEM)
    return pl.pallas_call(
        score_kernel,
        out_shape=jax.ShapeDtypeStruct((DP, 1, BLK), jnp.float32),
        in_specs=[vmem] * 3,
        out_specs=vmem,
        scratch_shapes=[pltpu.VMEM((BLK, BLK), jnp.float32)],
        compiler_params=params(),
        name="scores",
    )(tokens, gram, grams)


def total_kernel(r_ref, own_ref, gram_ref, o_ref):
    row = r_ref[0]
    for d in range(1, DP):
        row = row + r_ref[d]
    lane = lax.broadcasted_iota(jnp.int32, (1, BLK), 1)
    count = jnp.sum(jnp.where(lane == 4 * NB, row, 0.0))
    gram_ref[...] = own_ref[...] / count
    scale = jnp.zeros((1, BLK), jnp.float32)
    for k, levels in enumerate(LEVELS):
        scale = jnp.where(lane // NB == k, levels * levels / (OUT * BLK), scale)
    row = row * scale / count
    for t in range(NY * NC):
        o_ref[t] = row


def totals(rows, own):
    vmem = pl.BlockSpec(memory_space=pltpu.VMEM)
    return pl.pallas_call(
        total_kernel,
        out_shape=(
            jax.ShapeDtypeStruct((NB, ROWS, BLK), jnp.float32),
            jax.ShapeDtypeStruct((NY * NC, 1, BLK), jnp.float32),
        ),
        in_specs=[vmem, vmem],
        out_specs=(vmem, vmem),
        compiler_params=params(),
        name="totals",
    )(rows, own)


def spread_kernel(r_ref, o_ref, row_ref):
    n = NY * NC
    for t in range(n):
        row_ref[t : t + 1, :] = r_ref[t]
    lane = lax.broadcasted_iota(jnp.int32, (8, BLK), 1)
    source = lax.broadcasted_iota(jnp.int32, (8, BLK), 0)
    total = [jnp.zeros((1, BLK), jnp.float32)] * 4
    for h in range(n // 8):
        skewed = pltpu.roll(row_ref[h * 8 : (h + 1) * 8, :], 0, 1, stride=NB, stride_axis=0)
        for k in range(4):
            moved = pltpu.roll(skewed, (h * 8 * NB - k * NB) % BLK, 1)
            kept = jnp.where(lane // NB == source + h * 8, moved, 0.0)
            total[k] = total[k] + jnp.sum(kept, axis=0, keepdims=True)
    for k in range(4):
        o_ref[k : k + 1, :] = total[k]


def spread(rows):
    vmem = pl.BlockSpec(memory_space=pltpu.VMEM)
    return pl.pallas_call(
        spread_kernel,
        out_shape=jax.ShapeDtypeStruct((4, BLK), jnp.float32),
        in_specs=[vmem],
        out_specs=vmem,
        scratch_shapes=[pltpu.VMEM((NY * NC, BLK), jnp.float32)],
        compiler_params=params(),
        name="spread",
    )(rows)


CHUNKS = 2


def quant_kernel(bits_ref, x_ref, w_ref, own_ref, left_ref, right_ref, far_ref, o_ref, c_ref, u_ref, slab_ref):
    rows = w_ref.shape[0] // CHUNKS
    x = x_ref[0]

    def slab(p):
        for off, ref in enumerate((own_ref, right_ref, far_ref, left_ref)):
            base = pl.multiple_of(lax.rem(x + off, NX) * (NZ * ROWS), NZ * ROWS)
            chunk = jnp.concatenate([ref[i, p] for i in range(NZ)], axis=0)
            slab_ref[pl.ds(base, NZ * ROWS), :] = chunk
        return slab_ref[...]

    inv_diag = 1.0 / slab(NP - 1)[:, :NB].T
    p = 0
    for j in range(NB):
        first = j * BLK
        width = PANEL - first - BLK
        if width:
            for i in range(width // BLK):
                u = slab(p)
                p += 1
                high = u.astype(jnp.bfloat16)
                low = (u - high.astype(jnp.float32)).astype(jnp.bfloat16)
                cols = slice(i * BLK, (i + 1) * BLK)
                u_ref[0:BLK, cols] = high
                u_ref[BLK : 2 * BLK, cols] = high
                u_ref[2 * BLK : 3 * BLK, cols] = low
        bits = bits_ref[j]
        levels = jnp.where(bits == 2, 2.0, jnp.where(bits == 3, 4.0, jnp.where(bits == 4, 8.0, 128.0)))
        half = levels - 0.5
        for h in range(CHUNKS):
            part = slice(h * rows, (h + 1) * rows)
            if j == 0:
                c = w_ref[part, :BLK].astype(jnp.float32)
            else:
                c = c_ref[part, first : first + BLK]
            step = (jnp.max(jnp.abs(c), axis=1, keepdims=True) + 1e-6) / half
            u = c * (1.0 / step)
            q = step * jnp.clip(u - sine_over_two_pi(u), -levels, levels - 1.0)
            o_ref[part, first : first + BLK] = q.astype(jnp.bfloat16)
            if width:
                e = (c - q) * inv_diag[j : j + 1, :]
                high = e.astype(jnp.bfloat16)
                low = (e - high.astype(jnp.float32)).astype(jnp.bfloat16)
                lhs = jnp.concatenate([high, low, high], axis=1)
                update = jnp.dot(lhs, u_ref[:, :width], preferred_element_type=jnp.float32)
                if j == 0:
                    rest = w_ref[part, BLK:].astype(jnp.float32)
                else:
                    rest = c_ref[part, first + BLK :]
                c_ref[part, first + BLK :] = rest - update


def quantize(bits, x, weight, factor):
    rows = weight.shape[0]
    return pl.pallas_call(
        quant_kernel,
        out_shape=jax.ShapeDtypeStruct((rows, PANEL), jnp.bfloat16),
        in_specs=[
            pl.BlockSpec(memory_space=pltpu.SMEM),
            pl.BlockSpec(memory_space=pltpu.SMEM),
        ]
        + [pl.BlockSpec(memory_space=pltpu.VMEM)] * 5,
        out_specs=pl.BlockSpec(memory_space=pltpu.VMEM),
        scratch_shapes=[
            pltpu.VMEM((rows, PANEL), jnp.float32),
            pltpu.VMEM((3 * BLK, PANEL - BLK), jnp.bfloat16),
            pltpu.VMEM((BLK, BLK), jnp.float32),
        ],
        compiler_params=params(),
        name="quantize",
    )(bits, x, weight, *factor)


def exchange(pieces, axes):
    return lax.all_to_all(pieces, axes, 0, 0, tiled=False)


def shift_x(piece, by):
    return lax.ppermute(piece, "x", [(i, (i + by) % NX) for i in range(NX)])


def per_device(activations, token_ids, weight, inv_chol, bit_widths):
    dp = ("x", "z")
    tensor = ("y", "c")
    tokens = token_ids.reshape(1, -1)
    x = lax.axis_index("x").reshape(1).astype(jnp.int32)
    first = (lax.axis_index(dp) * ROWS).reshape(1).astype(jnp.int32)
    partial = gram_partial(tokens, activations)
    rows = exchange(partial, "x")
    grams = error_grams(weight)
    packed = sum_x(first, inv_chol, rows)
    over_z = exchange(packed, "z")
    own, copies = sum_z(over_z)
    gram = exchange(copies, dp)
    mine, _ = lax.optimization_barrier((over_z, copies))
    mine = mine[:, :NP]
    left = shift_x(mine, 1)
    right = shift_x(mine, -1)
    row = scores(tokens, gram, grams)
    left_late, _ = lax.optimization_barrier((left, row))
    row = exchange(row, dp)
    far = shift_x(left_late, 1)
    gram_out, row = totals(row, own)
    rows = exchange(row, tensor)
    quantized = quantize(bit_widths, x, weight, (mine, left, right, far))
    block_errors = spread(rows).T
    return quantized, gram_out, block_errors


def solution(mesh):
    fine = Mesh(mesh.devices.reshape(NX, NZ, NY, NC), ("x", "z", "y", "c"))
    dp = ("x", "z")
    tensor = ("y", "c")
    placed = (P(dp, tensor), P(dp), P(dp, tensor), P(tensor, dp, None), P(tensor))
    return jax.shard_map(
        per_device,
        mesh=fine,
        in_specs=placed,
        out_specs=(P(dp, tensor), P(tensor, dp, None), P()),
        check_vma=False,
    )
```

```python
import jax
import jax.numpy as jnp
from jax import lax
from jax.experimental import pallas as pl
from jax.experimental.pallas import tpu as pltpu
from jax.sharding import Mesh, PartitionSpec as P

OUT = 16384
BLK = 128
PANEL = 1024
NB = 8
DP = 32
ROWS = BLK // DP
NX, NZ, NY, NC = 4, 8, 8, 2
PAIRS = [(j, c) for j in range(NB) for c in range(j + 1, NB)]
NP = len(PAIRS) + 1
PAD = 128004
LEVELS = (2.0, 4.0, 8.0, 128.0)

SIN = (
    0.9999996039231652,
    -6.579691570100355,
    12.986436001995736,
    -12.188101551479916,
    6.558042314696102,
    -1.9530321174789678,
)


def sine_over_two_pi(u):
    r = u - jnp.round(u)
    z = r * r
    p = SIN[-1] * z + SIN[-2]
    for a in SIN[-3::-1]:
        p = p * z + a
    return p * r


def params(*semantics):
    return pltpu.CompilerParams(dimension_semantics=semantics, vmem_limit_bytes=56 << 20)


def gram_kernel(tok_ref, a_ref, o_ref):
    live = jnp.where(tok_ref[...] != PAD, 1.0, 0.0).astype(jnp.bfloat16)
    for b in range(NB):
        x = a_ref[:, b * BLK : (b + 1) * BLK]
        g = jnp.dot(x.T * live, x, preferred_element_type=jnp.float32)
        for d in range(DP):
            o_ref[d // NZ, d % NZ, b] = g[d * ROWS : (d + 1) * ROWS]


def gram_partial(tokens, activations):
    vmem = pl.BlockSpec(memory_space=pltpu.VMEM)
    return pl.pallas_call(
        gram_kernel,
        out_shape=pltpu.VMEM((NX, NZ, NB, ROWS, BLK), jnp.float32),
        in_specs=[vmem, vmem],
        out_specs=vmem,
        compiler_params=params(),
        name="gram_partial",
    )(tokens, activations)


def sum_x_kernel(first_ref, f_ref, g_ref, o_ref):
    lane = lax.broadcasted_iota(jnp.int32, (ROWS, BLK), 1)
    row = lax.broadcasted_iota(jnp.int32, (ROWS, BLK), 0)
    on_diag = lane == row + first_ref[0]
    diag = jnp.zeros((ROWS, BLK), jnp.float32)
    for j in range(NB):
        tile = f_ref[j, :, j * BLK : (j + 1) * BLK]
        value = jnp.sum(jnp.where(on_diag, tile, 0.0), axis=1, keepdims=True)
        diag = jnp.where(lane == j, value, diag)
    for i in range(NZ):
        o_ref[i, NP - 1] = diag
    for p, (j, c) in enumerate(PAIRS):
        tile = f_ref[j, :, c * BLK : (c + 1) * BLK]
        for i in range(NZ):
            o_ref[i, p] = tile
    for i in range(NZ):
        total = g_ref[0, i]
        for x in range(1, NX):
            total = total + g_ref[x, i]
        o_ref[i, NP:] = total


def sum_x(first, factor, received):
    vmem = pl.BlockSpec(memory_space=pltpu.VMEM)
    return pl.pallas_call(
        sum_x_kernel,
        out_shape=jax.ShapeDtypeStruct((NZ, NP + NB, ROWS, BLK), jnp.float32),
        in_specs=[pl.BlockSpec(memory_space=pltpu.SMEM), vmem, vmem],
        out_specs=vmem,
        compiler_params=params(),
        name="sum_x",
    )(first, factor, received)


def sum_z_kernel(g_ref, own_ref, o_ref):
    total = g_ref[0, NP:]
    for i in range(1, NZ):
        total = total + g_ref[i, NP:]
    own_ref[...] = total
    for d in range(DP):
        o_ref[d] = total


def sum_z(received):
    vmem = pl.BlockSpec(memory_space=pltpu.VMEM)
    return pl.pallas_call(
        sum_z_kernel,
        out_shape=(
            jax.ShapeDtypeStruct((NB, ROWS, BLK), jnp.float32),
            jax.ShapeDtypeStruct((DP, NB, ROWS, BLK), jnp.float32),
        ),
        in_specs=[vmem],
        out_specs=(vmem, vmem),
        compiler_params=params(),
        name="sum_z",
    )(received)


def error_kernel(w_ref, o_ref):
    w = w_ref[...].astype(jnp.float32)
    bound = jnp.max(jnp.abs(w), axis=1, keepdims=True) + 1e-6
    unit = w * (1.0 / bound)
    for k, levels in enumerate(LEVELS):
        u = unit * (levels - 0.5)
        smooth = jnp.clip(u - sine_over_two_pi(u), -levels, levels - 1.0)
        e = (w - (bound * (1.0 / (levels - 0.5))) * smooth).astype(jnp.bfloat16)
        s = lax.dot_general(e, e, (((0,), (0,)), ((), ())), preferred_element_type=jnp.float32)
        for d in range(DP):
            o_ref[0, k, d] = s[d * ROWS : (d + 1) * ROWS]


def error_grams(weight):
    rows = weight.shape[0]
    return pl.pallas_call(
        error_kernel,
        out_shape=jax.ShapeDtypeStruct((NB, 4, DP, ROWS, BLK), jnp.float32),
        grid=(NB,),
        in_specs=[pl.BlockSpec((rows, BLK), lambda b: (0, b))],
        out_specs=pl.BlockSpec((1, 4, DP, ROWS, BLK), lambda b: (b, 0, 0, 0, 0)),
        compiler_params=params("arbitrary"),
        name="error_grams",
    )(weight)


def score_kernel(tok_ref, g_ref, s_ref, o_ref, row_ref):
    row_ref[...] = jnp.zeros((BLK, BLK), jnp.float32)
    live = jnp.where(tok_ref[...] != PAD, 1.0, 0.0)
    row_ref[4 * NB : 4 * NB + 1, :] = sum(live[:, i : i + BLK] for i in range(0, live.shape[1], BLK))
    for b in range(NB):
        for k in range(4):
            acc = g_ref[0, b] * s_ref[b, k, 0]
            for d in range(1, DP):
                acc = acc + g_ref[d, b] * s_ref[b, k, d]
            row_ref[k * NB + b : k * NB + b + 1, :] = jnp.sum(acc, axis=0, keepdims=True)
    row = jnp.sum(row_ref[...].T, axis=0, keepdims=True)
    for d in range(DP):
        o_ref[d] = row


def scores(tokens, gram, grams):
    vmem = pl.BlockSpec(memory_space=pltpu.VMEM)
    return pl.pallas_call(
        score_kernel,
        out_shape=jax.ShapeDtypeStruct((DP, 1, BLK), jnp.float32),
        in_specs=[vmem] * 3,
        out_specs=vmem,
        scratch_shapes=[pltpu.VMEM((BLK, BLK), jnp.float32)],
        compiler_params=params(),
        name="scores",
    )(tokens, gram, grams)


def total_kernel(r_ref, own_ref, gram_ref, o_ref):
    row = r_ref[0]
    for d in range(1, DP):
        row = row + r_ref[d]
    lane = lax.broadcasted_iota(jnp.int32, (1, BLK), 1)
    count = jnp.sum(jnp.where(lane == 4 * NB, row, 0.0))
    gram_ref[...] = own_ref[...] / count
    scale = jnp.zeros((1, BLK), jnp.float32)
    for k, levels in enumerate(LEVELS):
        scale = jnp.where(lane // NB == k, levels * levels / (OUT * BLK), scale)
    row = row * scale / count
    for t in range(NY * NC):
        o_ref[t] = row


def totals(rows, own):
    vmem = pl.BlockSpec(memory_space=pltpu.VMEM)
    return pl.pallas_call(
        total_kernel,
        out_shape=(
            jax.ShapeDtypeStruct((NB, ROWS, BLK), jnp.float32),
            jax.ShapeDtypeStruct((NY * NC, 1, BLK), jnp.float32),
        ),
        in_specs=[vmem, vmem],
        out_specs=(vmem, vmem),
        compiler_params=params(),
        name="totals",
    )(rows, own)


def spread_kernel(r_ref, o_ref, row_ref):
    n = NY * NC
    for t in range(n):
        row_ref[t : t + 1, :] = r_ref[t]
    lane = lax.broadcasted_iota(jnp.int32, (8, BLK), 1)
    source = lax.broadcasted_iota(jnp.int32, (8, BLK), 0)
    total = [jnp.zeros((1, BLK), jnp.float32)] * 4
    for h in range(n // 8):
        skewed = pltpu.roll(row_ref[h * 8 : (h + 1) * 8, :], 0, 1, stride=NB, stride_axis=0)
        for k in range(4):
            moved = pltpu.roll(skewed, (h * 8 * NB - k * NB) % BLK, 1)
            kept = jnp.where(lane // NB == source + h * 8, moved, 0.0)
            total[k] = total[k] + jnp.sum(kept, axis=0, keepdims=True)
    for k in range(4):
        o_ref[k : k + 1, :] = total[k]


def spread(rows):
    vmem = pl.BlockSpec(memory_space=pltpu.VMEM)
    return pl.pallas_call(
        spread_kernel,
        out_shape=jax.ShapeDtypeStruct((4, BLK), jnp.float32),
        in_specs=[vmem],
        out_specs=vmem,
        scratch_shapes=[pltpu.VMEM((NY * NC, BLK), jnp.float32)],
        compiler_params=params(),
        name="spread",
    )(rows)


CHUNKS = 2


def quant_kernel(bits_ref, x_ref, w_ref, own_ref, left_ref, right_ref, far_ref, o_ref, c_ref, u_ref, slab_ref):
    rows = w_ref.shape[0] // CHUNKS
    x = x_ref[0]

    def slab(p):
        for off, ref in enumerate((own_ref, right_ref, far_ref, left_ref)):
            base = pl.multiple_of(lax.rem(x + off, NX) * (NZ * ROWS), NZ * ROWS)
            chunk = jnp.concatenate([ref[i, p] for i in range(NZ)], axis=0)
            slab_ref[pl.ds(base, NZ * ROWS), :] = chunk
        return slab_ref[...]

    inv_diag = 1.0 / slab(NP - 1)[:, :NB].T
    p = 0
    for j in range(NB):
        first = j * BLK
        width = PANEL - first - BLK
        if width:
            for i in range(width // BLK):
                u = slab(p)
                p += 1
                high = u.astype(jnp.bfloat16)
                low = (u - high.astype(jnp.float32)).astype(jnp.bfloat16)
                cols = slice(i * BLK, (i + 1) * BLK)
                u_ref[0:BLK, cols] = high
                u_ref[BLK : 2 * BLK, cols] = high
                u_ref[2 * BLK : 3 * BLK, cols] = low
        bits = bits_ref[j]
        levels = jnp.where(bits == 2, 2.0, jnp.where(bits == 3, 4.0, jnp.where(bits == 4, 8.0, 128.0)))
        half = levels - 0.5
        for h in range(CHUNKS):
            part = slice(h * rows, (h + 1) * rows)
            if j == 0:
                c = w_ref[part, :BLK].astype(jnp.float32)
            else:
                c = c_ref[part, first : first + BLK]
            step = (jnp.max(jnp.abs(c), axis=1, keepdims=True) + 1e-6) / half
            u = c * (1.0 / step)
            q = step * jnp.clip(u - sine_over_two_pi(u), -levels, levels - 1.0)
            o_ref[part, first : first + BLK] = q.astype(jnp.bfloat16)
            if width:
                e = (c - q) * inv_diag[j : j + 1, :]
                high = e.astype(jnp.bfloat16)
                low = (e - high.astype(jnp.float32)).astype(jnp.bfloat16)
                lhs = jnp.concatenate([high, low, high], axis=1)
                update = jnp.dot(lhs, u_ref[:, :width], preferred_element_type=jnp.float32)
                if j == 0:
                    rest = w_ref[part, BLK:].astype(jnp.float32)
                else:
                    rest = c_ref[part, first + BLK :]
                c_ref[part, first + BLK :] = rest - update


def quantize(bits, x, weight, factor):
    rows = weight.shape[0]
    return pl.pallas_call(
        quant_kernel,
        out_shape=jax.ShapeDtypeStruct((rows, PANEL), jnp.bfloat16),
        in_specs=[
            pl.BlockSpec(memory_space=pltpu.SMEM),
            pl.BlockSpec(memory_space=pltpu.SMEM),
        ]
        + [pl.BlockSpec(memory_space=pltpu.VMEM)] * 5,
        out_specs=pl.BlockSpec(memory_space=pltpu.VMEM),
        scratch_shapes=[
            pltpu.VMEM((rows, PANEL), jnp.float32),
            pltpu.VMEM((3 * BLK, PANEL - BLK), jnp.bfloat16),
            pltpu.VMEM((BLK, BLK), jnp.float32),
        ],
        compiler_params=params(),
        name="quantize",
    )(bits, x, weight, *factor)


def exchange(pieces, axes):
    return lax.all_to_all(pieces, axes, 0, 0, tiled=False)


def shift_x(piece, by):
    return lax.ppermute(piece, "x", [(i, (i + by) % NX) for i in range(NX)])


def near(array):
    return pltpu.with_memory_space_constraint(array, pltpu.VMEM)


def per_device(activations, token_ids, weight, inv_chol, bit_widths):
    dp = ("x", "z")
    tensor = ("y", "c")
    tokens = token_ids.reshape(1, -1)
    x = lax.axis_index("x").reshape(1).astype(jnp.int32)
    first = (lax.axis_index(dp) * ROWS).reshape(1).astype(jnp.int32)
    partial = gram_partial(tokens, activations)
    rows = exchange(partial, "x")
    grams = error_grams(weight)
    packed = sum_x(first, inv_chol, near(rows))
    over_z = exchange(packed, "z")
    own, copies = sum_z(near(over_z))
    gram = exchange(copies, dp)
    mine, _ = lax.optimization_barrier((over_z, copies))
    mine = mine[:, :NP]
    left = shift_x(mine, 1)
    right = shift_x(mine, -1)
    row = scores(tokens, near(gram), near(grams))
    left_late, _ = lax.optimization_barrier((left, row))
    row = exchange(row, dp)
    far = shift_x(left_late, 1)
    gram_out, row = totals(near(row), near(own))
    rows = exchange(row, tensor)
    quantized = quantize(bit_widths, x, weight, tuple(map(near, (mine, left, right, far))))
    block_errors = spread(near(rows)).T
    return quantized, gram_out, block_errors


def solution(mesh):
    fine = Mesh(mesh.devices.reshape(NX, NZ, NY, NC), ("x", "z", "y", "c"))
    dp = ("x", "z")
    tensor = ("y", "c")
    placed = (P(dp, tensor), P(dp), P(dp, tensor), P(tensor, dp, None), P(tensor))
    return jax.shard_map(
        per_device,
        mesh=fine,
        in_specs=placed,
        out_specs=(P(dp, tensor), P(tensor, dp, None), P()),
        check_vma=False,
    )
```

```python
import jax
import jax.numpy as jnp
from jax import lax
from jax.experimental import pallas as pl
from jax.experimental.pallas import tpu as pltpu
from jax.sharding import Mesh, PartitionSpec as P

OUT = 16384
BLK = 128
PANEL = 1024
NB = 8
DP = 32
ROWS = BLK // DP
NX, NZ, NY, NC = 4, 8, 8, 2
NT = NY * NC
PAIRS = [(j, c) for j in range(NB) for c in range(j + 1, NB)]
NP = len(PAIRS) + 1
HB = NB // 2
GT = HB + 1
PAD = 128004
LEVELS = (2.0, 4.0, 8.0, 128.0)

SIN = (
    0.9999996039231652,
    -6.579691570100355,
    12.986436001995736,
    -12.188101551479916,
    6.558042314696102,
    -1.9530321174789678,
)


def sine_over_two_pi(u):
    r = u - jnp.round(u)
    z = r * r
    p = SIN[-1] * z + SIN[-2]
    for a in SIN[-3::-1]:
        p = p * z + a
    return p * r


def params(*semantics):
    return pltpu.CompilerParams(dimension_semantics=semantics, vmem_limit_bytes=56 << 20)


def gram_kernel(tok_ref, a_ref, o_ref):
    live = jnp.where(tok_ref[...] != PAD, 1.0, 0.0).astype(jnp.bfloat16)
    row = lax.broadcasted_iota(jnp.int32, (BLK, BLK), 0)
    col = lax.broadcasted_iota(jnp.int32, (BLK, BLK), 1)
    diag = jnp.zeros((BLK, BLK), jnp.float32)

    def gram(b):
        x = a_ref[:, b * BLK : (b + 1) * BLK]
        return jnp.dot(x.T * live, x, preferred_element_type=jnp.float32)

    def put(g, tile):
        for d in range(DP):
            o_ref[d // NZ, d % NZ, tile] = g[d * ROWS : (d + 1) * ROWS]

    for b in range(HB):
        lower = gram(b + HB)
        put(jnp.where(col >= row, gram(b), lower), b)
        value = jnp.sum(jnp.where(col == row, lower, 0.0), axis=1, keepdims=True)
        diag = jnp.where(col == b + HB, value, diag)
    put(diag, HB)


def gram_partial(tokens, activations):
    vmem = pl.BlockSpec(memory_space=pltpu.VMEM)
    return pl.pallas_call(
        gram_kernel,
        out_shape=pltpu.VMEM((NX, NZ, GT, ROWS, BLK), jnp.float32),
        in_specs=[vmem, vmem],
        out_specs=vmem,
        compiler_params=params(),
        name="gram_partial",
    )(tokens, activations)


def sum_x_kernel(first_ref, f_ref, g_ref, o_ref):
    lane = lax.broadcasted_iota(jnp.int32, (ROWS, BLK), 1)
    row = lax.broadcasted_iota(jnp.int32, (ROWS, BLK), 0)
    on_diag = lane == row + first_ref[0]
    diag = jnp.zeros((ROWS, BLK), jnp.float32)
    for j in range(NB):
        tile = f_ref[j, :, j * BLK : (j + 1) * BLK]
        value = jnp.sum(jnp.where(on_diag, tile, 0.0), axis=1, keepdims=True)
        diag = jnp.where(lane == j, value, diag)
    for i in range(NZ):
        o_ref[i, NP - 1] = diag
    for p, (j, c) in enumerate(PAIRS):
        tile = f_ref[j, :, c * BLK : (c + 1) * BLK]
        for i in range(NZ):
            o_ref[i, p] = tile
    for i in range(NZ):
        total = g_ref[0, i]
        for x in range(1, NX):
            total = total + g_ref[x, i]
        o_ref[i, NP:] = total


def sum_x(first, factor, received):
    vmem = pl.BlockSpec(memory_space=pltpu.VMEM)
    return pl.pallas_call(
        sum_x_kernel,
        out_shape=jax.ShapeDtypeStruct((NZ, NP + GT, ROWS, BLK), jnp.float32),
        in_specs=[pl.BlockSpec(memory_space=pltpu.SMEM), vmem, vmem],
        out_specs=vmem,
        compiler_params=params(),
        name="sum_x",
    )(first, factor, received)


def sum_z_kernel(g_ref, own_ref, o_ref):
    total = g_ref[0, NP:]
    for i in range(1, NZ):
        total = total + g_ref[i, NP:]
    own_ref[...] = total
    for d in range(DP):
        o_ref[d] = total


def sum_z(received):
    vmem = pl.BlockSpec(memory_space=pltpu.VMEM)
    return pl.pallas_call(
        sum_z_kernel,
        out_shape=(
            jax.ShapeDtypeStruct((GT, ROWS, BLK), jnp.float32),
            jax.ShapeDtypeStruct((DP, GT, ROWS, BLK), jnp.float32),
        ),
        in_specs=[vmem],
        out_specs=(vmem, vmem),
        compiler_params=params(),
        name="sum_z",
    )(received)


def error_kernel(w_ref, o_ref, d_ref):
    b = pl.program_id(0)
    row = lax.broadcasted_iota(jnp.int32, (BLK, BLK), 0)
    col = lax.broadcasted_iota(jnp.int32, (BLK, BLK), 1)
    upper = jnp.where(col > row, 2.0, jnp.where(col == row, 1.0, 0.0))
    lower = jnp.where(col < row, 2.0, 0.0)
    weight = jnp.where(b < HB, upper, lower)
    w = w_ref[...].astype(jnp.float32)
    bound = jnp.max(jnp.abs(w), axis=1, keepdims=True) + 1e-6
    unit = w * (1.0 / bound)
    for k, levels in enumerate(LEVELS):
        u = unit * (levels - 0.5)
        smooth = jnp.clip(u - sine_over_two_pi(u), -levels, levels - 1.0)
        e = (w - (bound * (1.0 / (levels - 0.5))) * smooth).astype(jnp.bfloat16)
        s = lax.dot_general(e, e, (((0,), (0,)), ((), ())), preferred_element_type=jnp.float32)
        value = jnp.sum(jnp.where(col == row, s, 0.0), axis=1, keepdims=True)
        diag = jnp.where((col == b) & (b >= HB), value, 0.0)
        s = s * weight
        for d in range(DP):
            part = slice(d * ROWS, (d + 1) * ROWS)
            o_ref[0, k, d] = s[part]
            before = jnp.where(b == 0, 0.0, d_ref[k, d])
            d_ref[k, d] = before + diag[part]


def error_grams(weight):
    rows = weight.shape[0]
    return pl.pallas_call(
        error_kernel,
        out_shape=(
            jax.ShapeDtypeStruct((NB, 4, DP, ROWS, BLK), jnp.float32),
            jax.ShapeDtypeStruct((4, DP, ROWS, BLK), jnp.float32),
        ),
        grid=(NB,),
        in_specs=[pl.BlockSpec((rows, BLK), lambda b: (0, b))],
        out_specs=(
            pl.BlockSpec((1, 4, DP, ROWS, BLK), lambda b: (b, 0, 0, 0, 0)),
            pl.BlockSpec((4, DP, ROWS, BLK), lambda b: (0, 0, 0, 0)),
        ),
        compiler_params=params("arbitrary"),
        name="error_grams",
    )(weight)


def score_kernel(tok_ref, g_ref, s_ref, d_ref, o_ref, row_ref):
    row_ref[...] = jnp.zeros((BLK, BLK), jnp.float32)
    live = jnp.where(tok_ref[...] != PAD, 1.0, 0.0)
    row_ref[4 * NB : 4 * NB + 1, :] = sum(live[:, i : i + BLK] for i in range(0, live.shape[1], BLK))
    diagonals = jnp.zeros((1, BLK), jnp.float32)
    for k in range(4):
        for b in range(NB):
            acc = g_ref[0, b % HB] * s_ref[b, k, 0]
            for d in range(1, DP):
                acc = acc + g_ref[d, b % HB] * s_ref[b, k, d]
            row_ref[k * NB + b : k * NB + b + 1, :] = jnp.sum(acc, axis=0, keepdims=True)
        acc = g_ref[0, HB] * d_ref[k, 0]
        for d in range(1, DP):
            acc = acc + g_ref[d, HB] * d_ref[k, d]
        acc = jnp.sum(acc, axis=0, keepdims=True)
        diagonals = diagonals + (pltpu.roll(acc, k * NB, 1) if k else acc)
    row = jnp.sum(row_ref[...].T, axis=0, keepdims=True) + diagonals
    o_ref[...] = jnp.broadcast_to(row, o_ref.shape)


def scores(tokens, gram, grams, diagonals):
    vmem = pl.BlockSpec(memory_space=pltpu.VMEM)
    return pl.pallas_call(
        score_kernel,
        out_shape=jax.ShapeDtypeStruct((DP * NT, BLK), jnp.float32),
        in_specs=[vmem] * 4,
        out_specs=vmem,
        scratch_shapes=[pltpu.VMEM((BLK, BLK), jnp.float32)],
        compiler_params=params(),
        name="scores",
    )(tokens, gram, grams, diagonals)


def rows_kernel(first_ref, g_ref, own_ref, o_ref):
    first = first_ref[0]
    lane = lax.broadcasted_iota(jnp.int32, (ROWS, BLK), 1)
    mine = lax.broadcasted_iota(jnp.int32, (ROWS, BLK), 0) + first
    pick = jnp.where(
        lax.broadcasted_iota(jnp.int32, (8, BLK), 1) == lax.broadcasted_iota(jnp.int32, (8, BLK), 0) + first, 1.0, 0.0
    )
    for b in range(HB):
        square = jnp.concatenate([g_ref[d, b] for d in range(DP)], axis=0)
        turned = lax.dot_general(
            pick,
            square,
            (((1,), (1,)), ((), ())),
            precision=lax.Precision.HIGHEST,
            preferred_element_type=jnp.float32,
        )[:ROWS]
        own = own_ref[b]
        diag = jnp.sum(jnp.where(lane == b + HB, own_ref[HB], 0.0), axis=1, keepdims=True)
        o_ref[b] = jnp.where(lane >= mine, own, turned)
        o_ref[b + HB] = jnp.where(lane < mine, own, jnp.where(lane == mine, diag, turned))


def gram_rows(first, gram, own):
    vmem = pl.BlockSpec(memory_space=pltpu.VMEM)
    return pl.pallas_call(
        rows_kernel,
        out_shape=jax.ShapeDtypeStruct((NB, ROWS, BLK), jnp.float32),
        in_specs=[pl.BlockSpec(memory_space=pltpu.SMEM), vmem, vmem],
        out_specs=vmem,
        compiler_params=params(),
        name="gram_rows",
    )(first, gram, own)


def finish_kernel(r_ref, rows_ref, gram_ref, o_ref):
    total = r_ref[0:NT, :]
    for d in range(1, DP):
        total = total + r_ref[d * NT : (d + 1) * NT, :]
    lane = lax.broadcasted_iota(jnp.int32, (8, BLK), 1)
    source = lax.broadcasted_iota(jnp.int32, (8, BLK), 0)
    count = jnp.sum(jnp.where((lane == 4 * NB) & (source == 0), total[:8], 0.0))
    gram_ref[...] = rows_ref[...] / count
    sums = [jnp.zeros((1, BLK), jnp.float32)] * 4
    for h in range(NT // 8):
        skewed = pltpu.roll(total[h * 8 : (h + 1) * 8], 0, 1, stride=NB, stride_axis=0)
        for k in range(4):
            moved = pltpu.roll(skewed, (h * 8 * NB - k * NB) % BLK, 1)
            kept = jnp.where(lane // NB == source + h * 8, moved, 0.0)
            sums[k] = sums[k] + jnp.sum(kept, axis=0, keepdims=True)
    for k, levels in enumerate(LEVELS):
        o_ref[k : k + 1, :] = sums[k] * (levels * levels / (OUT * BLK)) / count


def finish(received, rows):
    vmem = pl.BlockSpec(memory_space=pltpu.VMEM)
    return pl.pallas_call(
        finish_kernel,
        out_shape=(
            jax.ShapeDtypeStruct((NB, ROWS, BLK), jnp.float32),
            jax.ShapeDtypeStruct((4, BLK), jnp.float32),
        ),
        in_specs=[vmem, vmem],
        out_specs=(vmem, vmem),
        compiler_params=params(),
        name="finish",
    )(received, rows)


CHUNKS = 2


def quant_kernel(bits_ref, x_ref, w_ref, own_ref, left_ref, right_ref, far_ref, o_ref, c_ref, u_ref, slab_ref):
    rows = w_ref.shape[0] // CHUNKS
    x = x_ref[0]

    def slab(p):
        for off, ref in enumerate((own_ref, right_ref, far_ref, left_ref)):
            base = pl.multiple_of(lax.rem(x + off, NX) * (NZ * ROWS), NZ * ROWS)
            chunk = jnp.concatenate([ref[i, p] for i in range(NZ)], axis=0)
            slab_ref[pl.ds(base, NZ * ROWS), :] = chunk
        return slab_ref[...]

    inv_diag = 1.0 / slab(NP - 1)[:, :NB].T
    p = 0
    for j in range(NB):
        first = j * BLK
        width = PANEL - first - BLK
        if width:
            for i in range(width // BLK):
                u = slab(p)
                p += 1
                high = u.astype(jnp.bfloat16)
                low = (u - high.astype(jnp.float32)).astype(jnp.bfloat16)
                cols = slice(i * BLK, (i + 1) * BLK)
                u_ref[0:BLK, cols] = high
                u_ref[BLK : 2 * BLK, cols] = high
                u_ref[2 * BLK : 3 * BLK, cols] = low
        bits = bits_ref[j]
        levels = jnp.where(bits == 2, 2.0, jnp.where(bits == 3, 4.0, jnp.where(bits == 4, 8.0, 128.0)))
        half = levels - 0.5
        for h in range(CHUNKS):
            part = slice(h * rows, (h + 1) * rows)
            if j == 0:
                c = w_ref[part, :BLK].astype(jnp.float32)
            else:
                c = c_ref[part, first : first + BLK]
            step = (jnp.max(jnp.abs(c), axis=1, keepdims=True) + 1e-6) / half
            u = c * (1.0 / step)
            q = step * jnp.clip(u - sine_over_two_pi(u), -levels, levels - 1.0)
            o_ref[part, first : first + BLK] = q.astype(jnp.bfloat16)
            if width:
                e = (c - q) * inv_diag[j : j + 1, :]
                high = e.astype(jnp.bfloat16)
                low = (e - high.astype(jnp.float32)).astype(jnp.bfloat16)
                lhs = jnp.concatenate([high, low, high], axis=1)
                update = jnp.dot(lhs, u_ref[:, :width], preferred_element_type=jnp.float32)
                if j == 0:
                    rest = w_ref[part, BLK:].astype(jnp.float32)
                else:
                    rest = c_ref[part, first + BLK :]
                c_ref[part, first + BLK :] = rest - update


def quantize(bits, x, weight, factor):
    rows = weight.shape[0]
    return pl.pallas_call(
        quant_kernel,
        out_shape=jax.ShapeDtypeStruct((rows, PANEL), jnp.bfloat16),
        in_specs=[
            pl.BlockSpec(memory_space=pltpu.SMEM),
            pl.BlockSpec(memory_space=pltpu.SMEM),
        ]
        + [pl.BlockSpec(memory_space=pltpu.VMEM)] * 5,
        out_specs=pl.BlockSpec(memory_space=pltpu.VMEM),
        scratch_shapes=[
            pltpu.VMEM((rows, PANEL), jnp.float32),
            pltpu.VMEM((3 * BLK, PANEL - BLK), jnp.bfloat16),
            pltpu.VMEM((BLK, BLK), jnp.float32),
        ],
        compiler_params=params(),
        name="quantize",
    )(bits, x, weight, *factor)


def exchange(pieces, axes):
    return lax.all_to_all(pieces, axes, 0, 0, tiled=False)


def shift_x(piece, by):
    return lax.ppermute(piece, "x", [(i, (i + by) % NX) for i in range(NX)])


def near(array):
    return pltpu.with_memory_space_constraint(array, pltpu.VMEM)


def per_device(activations, token_ids, weight, inv_chol, bit_widths):
    dp = ("x", "z")
    tensor = ("y", "c")
    tokens = token_ids.reshape(1, -1)
    x = lax.axis_index("x").reshape(1).astype(jnp.int32)
    first = (lax.axis_index(dp) * ROWS).reshape(1).astype(jnp.int32)
    partial = gram_partial(tokens, activations)
    rows = exchange(partial, "x")
    grams, diagonals = error_grams(weight)
    packed = sum_x(first, inv_chol, near(rows))
    over_z = exchange(packed, "z")
    own, copies = sum_z(near(over_z))
    gram = exchange(copies, dp)
    mine, _ = lax.optimization_barrier((over_z, copies))
    mine = mine[:, :NP]
    left = shift_x(mine, 1)
    right = shift_x(mine, -1)
    row = scores(tokens, near(gram), near(grams), near(diagonals))
    left_late, _ = lax.optimization_barrier((left, row))
    row = lax.all_to_all(row, dp + tensor, 0, 0, tiled=True)
    far = shift_x(left_late, 1)
    rows = gram_rows(first, near(gram), near(own))
    quantized = quantize(bit_widths, x, weight, tuple(map(near, (mine, left, right, far))))
    gram_out, block_errors = finish(near(row), near(rows))
    return quantized, gram_out, block_errors.T


def solution(mesh):
    fine = Mesh(mesh.devices.reshape(NX, NZ, NY, NC), ("x", "z", "y", "c"))
    dp = ("x", "z")
    tensor = ("y", "c")
    placed = (P(dp, tensor), P(dp), P(dp, tensor), P(tensor, dp, None), P(tensor))
    return jax.shard_map(
        per_device,
        mesh=fine,
        in_specs=placed,
        out_specs=(P(dp, tensor), P(tensor, dp, None), P()),
        check_vma=False,
    )
```

```python
import jax
import jax.numpy as jnp
from jax import lax
from jax.experimental import pallas as pl
from jax.experimental.pallas import tpu as pltpu
from jax.sharding import Mesh, PartitionSpec as P

OUT = 16384
BLK = 128
PANEL = 1024
NB = 8
DP = 32
ROWS = BLK // DP
NX, NZ, NY, NC = 4, 8, 8, 2
NT = NY * NC
PAIRS = [(j, c) for j in range(NB) for c in range(j + 1, NB)]
NP = len(PAIRS) + 1
HB = NB // 2
GT = HB + 1
PAD = 128004
LEVELS = (2.0, 4.0, 8.0, 128.0)

SIN = (
    0.9999996039231652,
    -6.579691570100355,
    12.986436001995736,
    -12.188101551479916,
    6.558042314696102,
    -1.9530321174789678,
)


def sine_over_two_pi(u):
    r = u - jnp.round(u)
    z = r * r
    p = SIN[-1] * z + SIN[-2]
    for a in SIN[-3::-1]:
        p = p * z + a
    return p * r


def params(*semantics):
    return pltpu.CompilerParams(dimension_semantics=semantics, vmem_limit_bytes=56 << 20)


def gram_kernel(x_ref, tok_ref, a_ref, *refs):
    outs, o_ref = refs[:NX], refs[NX]
    live = jnp.where(tok_ref[...] != PAD, 1.0, 0.0).astype(jnp.bfloat16)
    row = lax.broadcasted_iota(jnp.int32, (BLK, BLK), 0)
    col = lax.broadcasted_iota(jnp.int32, (BLK, BLK), 1)
    diag = jnp.zeros((BLK, BLK), jnp.float32)

    def gram(b):
        x = a_ref[:, b * BLK : (b + 1) * BLK]
        return jnp.dot(x.T * live, x, preferred_element_type=jnp.float32)

    def put(g, tile):
        for d in range(DP):
            o_ref[d // NZ, d % NZ, tile] = g[d * ROWS : (d + 1) * ROWS]

    for b in range(HB):
        lower = gram(b + HB)
        put(jnp.where(col >= row, gram(b), lower), b)
        value = jnp.sum(jnp.where(col == row, lower, 0.0), axis=1, keepdims=True)
        diag = jnp.where(col == b + HB, value, diag)
    put(diag, HB)
    for off in range(NX):
        outs[off][...] = o_ref[lax.rem(x_ref[0] + off, NX)]


def gram_partial(x, tokens, activations):
    vmem = pl.BlockSpec(memory_space=pltpu.VMEM)
    return pl.pallas_call(
        gram_kernel,
        out_shape=[jax.ShapeDtypeStruct((NZ, GT, ROWS, BLK), jnp.float32)] * NX,
        in_specs=[pl.BlockSpec(memory_space=pltpu.SMEM), vmem, vmem],
        out_specs=[vmem] * NX,
        scratch_shapes=[pltpu.VMEM((NX, NZ, GT, ROWS, BLK), jnp.float32)],
        compiler_params=params(),
        name="gram_partial",
    )(x, tokens, activations)


def pack_kernel(first_ref, f_ref, o_ref):
    lane = lax.broadcasted_iota(jnp.int32, (ROWS, BLK), 1)
    row = lax.broadcasted_iota(jnp.int32, (ROWS, BLK), 0)
    on_diag = lane == row + first_ref[0]
    diag = jnp.zeros((ROWS, BLK), jnp.float32)
    for j in range(NB):
        tile = f_ref[j, :, j * BLK : (j + 1) * BLK]
        value = jnp.sum(jnp.where(on_diag, tile, 0.0), axis=1, keepdims=True)
        diag = jnp.where(lane == j, value, diag)
    for i in range(NZ):
        o_ref[i, NP - 1] = diag
    for p, (j, c) in enumerate(PAIRS):
        tile = f_ref[j, :, c * BLK : (c + 1) * BLK]
        for i in range(NZ):
            o_ref[i, p] = tile


def pack(first, factor):
    vmem = pl.BlockSpec(memory_space=pltpu.VMEM)
    return pl.pallas_call(
        pack_kernel,
        out_shape=jax.ShapeDtypeStruct((NZ, NP, ROWS, BLK), jnp.float32),
        in_specs=[pl.BlockSpec(memory_space=pltpu.SMEM), vmem],
        out_specs=vmem,
        compiler_params=params(),
        name="pack",
    )(first, factor)


def sum_x_kernel(a_ref, b_ref, c_ref, d_ref, o_ref):
    o_ref[...] = (a_ref[...] + b_ref[...]) + (c_ref[...] + d_ref[...])


def sum_x(parts):
    vmem = pl.BlockSpec(memory_space=pltpu.VMEM)
    return pl.pallas_call(
        sum_x_kernel,
        out_shape=jax.ShapeDtypeStruct((NZ, GT, ROWS, BLK), jnp.float32),
        in_specs=[vmem] * NX,
        out_specs=vmem,
        compiler_params=params(),
        name="sum_x",
    )(*parts)


def sum_z_kernel(g_ref, own_ref, o_ref):
    total = g_ref[0]
    for i in range(1, NZ):
        total = total + g_ref[i]
    own_ref[...] = total
    for d in range(DP):
        o_ref[d] = total


def sum_z(received):
    vmem = pl.BlockSpec(memory_space=pltpu.VMEM)
    return pl.pallas_call(
        sum_z_kernel,
        out_shape=(
            pltpu.VMEM((GT, ROWS, BLK), jnp.float32),
            jax.ShapeDtypeStruct((DP, GT, ROWS, BLK), jnp.float32),
        ),
        in_specs=[vmem],
        out_specs=(vmem, vmem),
        compiler_params=params(),
        name="sum_z",
    )(received)


def error_kernel(w_ref, o_ref, d_ref):
    b = pl.program_id(0)
    row = lax.broadcasted_iota(jnp.int32, (BLK, BLK), 0)
    col = lax.broadcasted_iota(jnp.int32, (BLK, BLK), 1)
    upper = jnp.where(col > row, 2.0, jnp.where(col == row, 1.0, 0.0))
    lower = jnp.where(col < row, 2.0, 0.0)
    weight = jnp.where(b < HB, upper, lower)
    w = w_ref[...].astype(jnp.float32)
    bound = jnp.max(jnp.abs(w), axis=1, keepdims=True) + 1e-6
    unit = w * (1.0 / bound)
    for k, levels in enumerate(LEVELS):
        u = unit * (levels - 0.5)
        smooth = jnp.clip(u - sine_over_two_pi(u), -levels, levels - 1.0)
        e = (w - (bound * (1.0 / (levels - 0.5))) * smooth).astype(jnp.bfloat16)
        s = lax.dot_general(e, e, (((0,), (0,)), ((), ())), preferred_element_type=jnp.float32)
        value = jnp.sum(jnp.where(col == row, s, 0.0), axis=1, keepdims=True)
        diag = jnp.where((col == b) & (b >= HB), value, 0.0)
        s = s * weight
        for d in range(DP):
            part = slice(d * ROWS, (d + 1) * ROWS)
            o_ref[0, k, d] = s[part]
            before = jnp.where(b == 0, 0.0, d_ref[k, d])
            d_ref[k, d] = before + diag[part]


def error_grams(weight):
    rows = weight.shape[0]
    return pl.pallas_call(
        error_kernel,
        out_shape=(
            jax.ShapeDtypeStruct((NB, 4, DP, ROWS, BLK), jnp.float32),
            jax.ShapeDtypeStruct((4, DP, ROWS, BLK), jnp.float32),
        ),
        grid=(NB,),
        in_specs=[pl.BlockSpec((rows, BLK), lambda b: (0, b))],
        out_specs=(
            pl.BlockSpec((1, 4, DP, ROWS, BLK), lambda b: (b, 0, 0, 0, 0)),
            pl.BlockSpec((4, DP, ROWS, BLK), lambda b: (0, 0, 0, 0)),
        ),
        compiler_params=params("arbitrary"),
        name="error_grams",
    )(weight)


def score_kernel(tok_ref, g_ref, s_ref, d_ref, o_ref, row_ref):
    row_ref[...] = jnp.zeros((BLK, BLK), jnp.float32)
    live = jnp.where(tok_ref[...] != PAD, 1.0, 0.0)
    row_ref[4 * NB : 4 * NB + 1, :] = sum(live[:, i : i + BLK] for i in range(0, live.shape[1], BLK))
    diagonals = jnp.zeros((1, BLK), jnp.float32)
    for k in range(4):
        for b in range(NB):
            acc = g_ref[0, b % HB] * s_ref[b, k, 0]
            for d in range(1, DP):
                acc = acc + g_ref[d, b % HB] * s_ref[b, k, d]
            row_ref[k * NB + b : k * NB + b + 1, :] = jnp.sum(acc, axis=0, keepdims=True)
        acc = g_ref[0, HB] * d_ref[k, 0]
        for d in range(1, DP):
            acc = acc + g_ref[d, HB] * d_ref[k, d]
        acc = jnp.sum(acc, axis=0, keepdims=True)
        diagonals = diagonals + (pltpu.roll(acc, k * NB, 1) if k else acc)
    row = jnp.sum(row_ref[...].T, axis=0, keepdims=True) + diagonals
    for d in range(DP):
        o_ref[d] = row


def scores(tokens, gram, grams, diagonals):
    vmem = pl.BlockSpec(memory_space=pltpu.VMEM)
    return pl.pallas_call(
        score_kernel,
        out_shape=jax.ShapeDtypeStruct((DP, 1, BLK), jnp.float32),
        in_specs=[vmem] * 4,
        out_specs=vmem,
        scratch_shapes=[pltpu.VMEM((BLK, BLK), jnp.float32)],
        compiler_params=params(),
        name="scores",
    )(tokens, gram, grams, diagonals)


def rows_kernel(first_ref, g_ref, own_ref, o_ref):
    first = first_ref[0]
    lane = lax.broadcasted_iota(jnp.int32, (ROWS, BLK), 1)
    mine = lax.broadcasted_iota(jnp.int32, (ROWS, BLK), 0) + first
    pick = jnp.where(
        lax.broadcasted_iota(jnp.int32, (8, BLK), 1) == lax.broadcasted_iota(jnp.int32, (8, BLK), 0) + first, 1.0, 0.0
    )
    for b in range(HB):
        square = jnp.concatenate([g_ref[d, b] for d in range(DP)], axis=0)
        turned = lax.dot_general(
            pick,
            square,
            (((1,), (1,)), ((), ())),
            precision=lax.Precision.HIGHEST,
            preferred_element_type=jnp.float32,
        )[:ROWS]
        own = own_ref[b]
        diag = jnp.sum(jnp.where(lane == b + HB, own_ref[HB], 0.0), axis=1, keepdims=True)
        o_ref[b] = jnp.where(lane >= mine, own, turned)
        o_ref[b + HB] = jnp.where(lane < mine, own, jnp.where(lane == mine, diag, turned))


def gram_rows(first, gram, own):
    vmem = pl.BlockSpec(memory_space=pltpu.VMEM)
    return pl.pallas_call(
        rows_kernel,
        out_shape=pltpu.VMEM((NB, ROWS, BLK), jnp.float32),
        in_specs=[pl.BlockSpec(memory_space=pltpu.SMEM), vmem, vmem],
        out_specs=vmem,
        compiler_params=params(),
        name="gram_rows",
    )(first, gram, own)


def total_kernel(r_ref, own_ref, gram_ref, o_ref):
    row = r_ref[0]
    for d in range(1, DP):
        row = row + r_ref[d]
    lane = lax.broadcasted_iota(jnp.int32, (1, BLK), 1)
    count = jnp.sum(jnp.where(lane == 4 * NB, row, 0.0))
    gram_ref[...] = own_ref[...] / count
    scale = jnp.zeros((1, BLK), jnp.float32)
    for k, levels in enumerate(LEVELS):
        scale = jnp.where(lane // NB == k, levels * levels / (OUT * BLK), scale)
    row = row * scale / count
    for t in range(NT):
        o_ref[t] = row


def totals(rows, own):
    vmem = pl.BlockSpec(memory_space=pltpu.VMEM)
    return pl.pallas_call(
        total_kernel,
        out_shape=(
            jax.ShapeDtypeStruct((NB, ROWS, BLK), jnp.float32),
            jax.ShapeDtypeStruct((NT, 1, BLK), jnp.float32),
        ),
        in_specs=[vmem, vmem],
        out_specs=(vmem, vmem),
        compiler_params=params(),
        name="totals",
    )(rows, own)


def spread_kernel(r_ref, o_ref, row_ref):
    n = NT
    for t in range(n):
        row_ref[t : t + 1, :] = r_ref[t]
    lane = lax.broadcasted_iota(jnp.int32, (8, BLK), 1)
    source = lax.broadcasted_iota(jnp.int32, (8, BLK), 0)
    total = [jnp.zeros((1, BLK), jnp.float32)] * 4
    for h in range(n // 8):
        skewed = pltpu.roll(row_ref[h * 8 : (h + 1) * 8, :], 0, 1, stride=NB, stride_axis=0)
        for k in range(4):
            moved = pltpu.roll(skewed, (h * 8 * NB - k * NB) % BLK, 1)
            kept = jnp.where(lane // NB == source + h * 8, moved, 0.0)
            total[k] = total[k] + jnp.sum(kept, axis=0, keepdims=True)
    for k in range(4):
        o_ref[k : k + 1, :] = total[k]


def spread(rows):
    vmem = pl.BlockSpec(memory_space=pltpu.VMEM)
    return pl.pallas_call(
        spread_kernel,
        out_shape=jax.ShapeDtypeStruct((4, BLK), jnp.float32),
        in_specs=[vmem],
        out_specs=vmem,
        scratch_shapes=[pltpu.VMEM((NT, BLK), jnp.float32)],
        compiler_params=params(),
        name="spread",
    )(rows)


CHUNKS = 2


def quant_kernel(bits_ref, x_ref, w_ref, own_ref, left_ref, right_ref, far_ref, o_ref, c_ref, u_ref, slab_ref):
    rows = w_ref.shape[0] // CHUNKS
    x = x_ref[0]

    def slab(p):
        for off, ref in enumerate((own_ref, right_ref, far_ref, left_ref)):
            base = pl.multiple_of(lax.rem(x + off, NX) * (NZ * ROWS), NZ * ROWS)
            chunk = jnp.concatenate([ref[i, p] for i in range(NZ)], axis=0)
            slab_ref[pl.ds(base, NZ * ROWS), :] = chunk
        return slab_ref[...]

    inv_diag = 1.0 / slab(NP - 1)[:, :NB].T
    p = 0
    for j in range(NB):
        first = j * BLK
        width = PANEL - first - BLK
        if width:
            for i in range(width // BLK):
                u = slab(p)
                p += 1
                high = u.astype(jnp.bfloat16)
                low = (u - high.astype(jnp.float32)).astype(jnp.bfloat16)
                cols = slice(i * BLK, (i + 1) * BLK)
                u_ref[0:BLK, cols] = high
                u_ref[BLK : 2 * BLK, cols] = high
                u_ref[2 * BLK : 3 * BLK, cols] = low
        bits = bits_ref[j]
        levels = jnp.where(bits == 2, 2.0, jnp.where(bits == 3, 4.0, jnp.where(bits == 4, 8.0, 128.0)))
        half = levels - 0.5
        for h in range(CHUNKS):
            part = slice(h * rows, (h + 1) * rows)
            if j == 0:
                c = w_ref[part, :BLK].astype(jnp.float32)
            else:
                c = c_ref[part, first : first + BLK]
            step = (jnp.max(jnp.abs(c), axis=1, keepdims=True) + 1e-6) / half
            u = c * (1.0 / step)
            q = step * jnp.clip(u - sine_over_two_pi(u), -levels, levels - 1.0)
            o_ref[part, first : first + BLK] = q.astype(jnp.bfloat16)
            if width:
                e = (c - q) * inv_diag[j : j + 1, :]
                high = e.astype(jnp.bfloat16)
                low = (e - high.astype(jnp.float32)).astype(jnp.bfloat16)
                lhs = jnp.concatenate([high, low, high], axis=1)
                update = jnp.dot(lhs, u_ref[:, :width], preferred_element_type=jnp.float32)
                if j == 0:
                    rest = w_ref[part, BLK:].astype(jnp.float32)
                else:
                    rest = c_ref[part, first + BLK :]
                c_ref[part, first + BLK :] = rest - update


def quantize(bits, x, weight, factor):
    rows = weight.shape[0]
    return pl.pallas_call(
        quant_kernel,
        out_shape=jax.ShapeDtypeStruct((rows, PANEL), jnp.bfloat16),
        in_specs=[
            pl.BlockSpec(memory_space=pltpu.SMEM),
            pl.BlockSpec(memory_space=pltpu.SMEM),
        ]
        + [pl.BlockSpec(memory_space=pltpu.VMEM)] * 5,
        out_specs=pl.BlockSpec(memory_space=pltpu.VMEM),
        scratch_shapes=[
            pltpu.VMEM((rows, PANEL), jnp.float32),
            pltpu.VMEM((3 * BLK, PANEL - BLK), jnp.bfloat16),
            pltpu.VMEM((BLK, BLK), jnp.float32),
        ],
        compiler_params=params(),
        name="quantize",
    )(bits, x, weight, *factor)


def exchange(pieces, axes):
    return lax.all_to_all(pieces, axes, 0, 0, tiled=False)


def shift_x(piece, by):
    return lax.ppermute(piece, "x", [(i, (i + by) % NX) for i in range(NX)])


def near(array):
    return pltpu.with_memory_space_constraint(array, pltpu.VMEM)


def per_device(activations, token_ids, weight, inv_chol, bit_widths):
    dp = ("x", "z")
    tensor = ("y", "c")
    tokens = token_ids.reshape(1, -1)
    x = lax.axis_index("x").reshape(1).astype(jnp.int32)
    first = (lax.axis_index(dp) * ROWS).reshape(1).astype(jnp.int32)
    packed = pack(first, inv_chol)
    mine = exchange(packed, "z")
    partial = gram_partial(x, tokens, activations)
    parts = [near(partial[0])]
    for off in range(1, NX):
        parts.append(near(shift_x(partial[off], off)))
    rows = sum_x(parts)
    mine, rows = lax.optimization_barrier((mine, rows))
    rows = exchange(rows, "z")
    left = shift_x(mine, 1)
    right = shift_x(mine, -1)
    own, copies = sum_z(near(rows))
    gram = exchange(copies, dp)
    grams, diagonals = error_grams(weight)
    row = scores(tokens, near(gram), near(grams), diagonals)
    left_late, _ = lax.optimization_barrier((left, row))
    row = exchange(row, dp)
    far = shift_x(left_late, 1)
    rows = gram_rows(first, near(gram), near(own))
    quantized = quantize(bit_widths, x, weight, tuple(map(near, (mine, left, right, far))))
    gram_out, row = totals(near(row), near(rows))
    row = exchange(row, tensor)
    block_errors = spread(near(row))
    return quantized, gram_out, block_errors.T


def solution(mesh):
    fine = Mesh(mesh.devices.reshape(NX, NZ, NY, NC), ("x", "z", "y", "c"))
    dp = ("x", "z")
    tensor = ("y", "c")
    placed = (P(dp, tensor), P(dp), P(dp, tensor), P(tensor, dp, None), P(tensor))
    return jax.shard_map(
        per_device,
        mesh=fine,
        in_specs=placed,
        out_specs=(P(dp, tensor), P(tensor, dp, None), P()),
        check_vma=False,
    )
```

```python
import jax
import jax.numpy as jnp
from jax import lax
from jax.experimental import pallas as pl
from jax.experimental.pallas import tpu as pltpu
from jax.sharding import Mesh, PartitionSpec as P

OUT = 16384
BLK = 128
PANEL = 1024
NB = 8
DP = 32
ROWS = BLK // DP
NX, NZ, NY, NC = 4, 8, 8, 2
NT = NY * NC
PAIRS = [(j, c) for j in range(NB) for c in range(j + 1, NB)]
NP = len(PAIRS) + 1
HB = NB // 2
GT = HB + 1
PAD = 128004
LEVELS = (2.0, 4.0, 8.0, 128.0)

SIN = (
    0.9999996039231652,
    -6.579691570100355,
    12.986436001995736,
    -12.188101551479916,
    6.558042314696102,
    -1.9530321174789678,
)


def sine_over_two_pi(u):
    r = u - jnp.round(u)
    z = r * r
    p = SIN[-1] * z + SIN[-2]
    for a in SIN[-3::-1]:
        p = p * z + a
    return p * r


def params(*semantics):
    return pltpu.CompilerParams(dimension_semantics=semantics, vmem_limit_bytes=56 << 20)


def gram_kernel(tok_ref, a_ref, o_ref):
    live = jnp.where(tok_ref[...] != PAD, 1.0, 0.0).astype(jnp.bfloat16)
    row = lax.broadcasted_iota(jnp.int32, (BLK, BLK), 0)
    col = lax.broadcasted_iota(jnp.int32, (BLK, BLK), 1)
    diag = jnp.zeros((BLK, BLK), jnp.float32)

    def gram(b):
        x = a_ref[:, b * BLK : (b + 1) * BLK]
        return jnp.dot(x.T * live, x, preferred_element_type=jnp.float32)

    def put(g, tile):
        for d in range(DP):
            o_ref[d // NZ, d % NZ, tile] = g[d * ROWS : (d + 1) * ROWS]

    for b in range(HB):
        lower = gram(b + HB)
        put(jnp.where(col >= row, gram(b), lower), b)
        value = jnp.sum(jnp.where(col == row, lower, 0.0), axis=1, keepdims=True)
        diag = jnp.where(col == b + HB, value, diag)
    put(diag, HB)


def gram_partial(tokens, activations):
    vmem = pl.BlockSpec(memory_space=pltpu.VMEM)
    return pl.pallas_call(
        gram_kernel,
        out_shape=pltpu.VMEM((NX, NZ, GT, ROWS, BLK), jnp.float32),
        in_specs=[vmem, vmem],
        out_specs=vmem,
        compiler_params=params(),
        name="gram_partial",
    )(tokens, activations)


def sum_x_kernel(first_ref, f_ref, g_ref, o_ref):
    lane = lax.broadcasted_iota(jnp.int32, (ROWS, BLK), 1)
    row = lax.broadcasted_iota(jnp.int32, (ROWS, BLK), 0)
    on_diag = lane == row + first_ref[0]
    diag = jnp.zeros((ROWS, BLK), jnp.float32)
    for j in range(NB):
        tile = f_ref[j, :, j * BLK : (j + 1) * BLK]
        value = jnp.sum(jnp.where(on_diag, tile, 0.0), axis=1, keepdims=True)
        diag = jnp.where(lane == j, value, diag)
    for i in range(NZ):
        o_ref[i, NP - 1] = diag
    for p, (j, c) in enumerate(PAIRS):
        tile = f_ref[j, :, c * BLK : (c + 1) * BLK]
        for i in range(NZ):
            o_ref[i, p] = tile
    for i in range(NZ):
        total = g_ref[0, i]
        for x in range(1, NX):
            total = total + g_ref[x, i]
        o_ref[i, NP:] = total


def sum_x(first, factor, received):
    vmem = pl.BlockSpec(memory_space=pltpu.VMEM)
    return pl.pallas_call(
        sum_x_kernel,
        out_shape=jax.ShapeDtypeStruct((NZ, NP + GT, ROWS, BLK), jnp.float32),
        in_specs=[pl.BlockSpec(memory_space=pltpu.SMEM), vmem, vmem],
        out_specs=vmem,
        compiler_params=params(),
        name="sum_x",
    )(first, factor, received)


def sum_z_kernel(g_ref, own_ref, o_ref):
    total = g_ref[0, NP:]
    for i in range(1, NZ):
        total = total + g_ref[i, NP:]
    own_ref[...] = total
    for d in range(DP):
        o_ref[d] = total


def sum_z(received):
    vmem = pl.BlockSpec(memory_space=pltpu.VMEM)
    return pl.pallas_call(
        sum_z_kernel,
        out_shape=(
            pltpu.VMEM((GT, ROWS, BLK), jnp.float32),
            jax.ShapeDtypeStruct((DP, GT, ROWS, BLK), jnp.float32),
        ),
        in_specs=[vmem],
        out_specs=(vmem, vmem),
        compiler_params=params(),
        name="sum_z",
    )(received)


def error_kernel(w_ref, o_ref, d_ref):
    b = pl.program_id(0)
    row = lax.broadcasted_iota(jnp.int32, (BLK, BLK), 0)
    col = lax.broadcasted_iota(jnp.int32, (BLK, BLK), 1)
    upper = jnp.where(col > row, 2.0, jnp.where(col == row, 1.0, 0.0))
    lower = jnp.where(col < row, 2.0, 0.0)
    weight = jnp.where(b < HB, upper, lower)
    w = w_ref[...].astype(jnp.float32)
    bound = jnp.max(jnp.abs(w), axis=1, keepdims=True) + 1e-6
    unit = w * (1.0 / bound)
    for k, levels in enumerate(LEVELS):
        u = unit * (levels - 0.5)
        smooth = jnp.clip(u - sine_over_two_pi(u), -levels, levels - 1.0)
        e = (w - (bound * (1.0 / (levels - 0.5))) * smooth).astype(jnp.bfloat16)
        s = lax.dot_general(e, e, (((0,), (0,)), ((), ())), preferred_element_type=jnp.float32)
        value = jnp.sum(jnp.where(col == row, s, 0.0), axis=1, keepdims=True)
        diag = jnp.where((col == b) & (b >= HB), value, 0.0)
        s = s * weight
        for d in range(DP):
            part = slice(d * ROWS, (d + 1) * ROWS)
            o_ref[0, k, d] = s[part]
            before = jnp.where(b == 0, 0.0, d_ref[k, d])
            d_ref[k, d] = before + diag[part]


def error_grams(weight):
    rows = weight.shape[0]
    return pl.pallas_call(
        error_kernel,
        out_shape=(
            jax.ShapeDtypeStruct((NB, 4, DP, ROWS, BLK), jnp.float32),
            jax.ShapeDtypeStruct((4, DP, ROWS, BLK), jnp.float32),
        ),
        grid=(NB,),
        in_specs=[pl.BlockSpec((rows, BLK), lambda b: (0, b))],
        out_specs=(
            pl.BlockSpec((1, 4, DP, ROWS, BLK), lambda b: (b, 0, 0, 0, 0)),
            pl.BlockSpec((4, DP, ROWS, BLK), lambda b: (0, 0, 0, 0)),
        ),
        compiler_params=params("arbitrary"),
        name="error_grams",
    )(weight)


def score_kernel(tok_ref, g_ref, s_ref, d_ref, o_ref, row_ref):
    row_ref[...] = jnp.zeros((BLK, BLK), jnp.float32)
    live = jnp.where(tok_ref[...] != PAD, 1.0, 0.0)
    row_ref[4 * NB : 4 * NB + 1, :] = sum(live[:, i : i + BLK] for i in range(0, live.shape[1], BLK))
    diagonals = jnp.zeros((1, BLK), jnp.float32)
    for k in range(4):
        for b in range(NB):
            acc = g_ref[0, b % HB] * s_ref[b, k, 0]
            for d in range(1, DP):
                acc = acc + g_ref[d, b % HB] * s_ref[b, k, d]
            row_ref[k * NB + b : k * NB + b + 1, :] = jnp.sum(acc, axis=0, keepdims=True)
        acc = g_ref[0, HB] * d_ref[k, 0]
        for d in range(1, DP):
            acc = acc + g_ref[d, HB] * d_ref[k, d]
        acc = jnp.sum(acc, axis=0, keepdims=True)
        diagonals = diagonals + (pltpu.roll(acc, k * NB, 1) if k else acc)
    row = jnp.sum(row_ref[...].T, axis=0, keepdims=True) + diagonals
    for d in range(DP):
        o_ref[d] = row


def scores(tokens, gram, grams, diagonals):
    vmem = pl.BlockSpec(memory_space=pltpu.VMEM)
    return pl.pallas_call(
        score_kernel,
        out_shape=jax.ShapeDtypeStruct((DP, 1, BLK), jnp.float32),
        in_specs=[vmem] * 4,
        out_specs=vmem,
        scratch_shapes=[pltpu.VMEM((BLK, BLK), jnp.float32)],
        compiler_params=params(),
        name="scores",
    )(tokens, gram, grams, diagonals)


def rows_kernel(first_ref, g_ref, own_ref, o_ref):
    first = first_ref[0]
    lane = lax.broadcasted_iota(jnp.int32, (ROWS, BLK), 1)
    mine = lax.broadcasted_iota(jnp.int32, (ROWS, BLK), 0) + first
    pick = jnp.where(
        lax.broadcasted_iota(jnp.int32, (8, BLK), 1) == lax.broadcasted_iota(jnp.int32, (8, BLK), 0) + first, 1.0, 0.0
    )
    for b in range(HB):
        square = jnp.concatenate([g_ref[d, b] for d in range(DP)], axis=0)
        turned = lax.dot_general(
            pick,
            square,
            (((1,), (1,)), ((), ())),
            precision=lax.Precision.HIGHEST,
            preferred_element_type=jnp.float32,
        )[:ROWS]
        own = own_ref[b]
        diag = jnp.sum(jnp.where(lane == b + HB, own_ref[HB], 0.0), axis=1, keepdims=True)
        o_ref[b] = jnp.where(lane >= mine, own, turned)
        o_ref[b + HB] = jnp.where(lane < mine, own, jnp.where(lane == mine, diag, turned))


def gram_rows(first, gram, own):
    vmem = pl.BlockSpec(memory_space=pltpu.VMEM)
    return pl.pallas_call(
        rows_kernel,
        out_shape=pltpu.VMEM((NB, ROWS, BLK), jnp.float32),
        in_specs=[pl.BlockSpec(memory_space=pltpu.SMEM), vmem, vmem],
        out_specs=vmem,
        compiler_params=params(),
        name="gram_rows",
    )(first, gram, own)


def total_kernel(r_ref, own_ref, gram_ref, o_ref):
    row = r_ref[0]
    for d in range(1, DP):
        row = row + r_ref[d]
    lane = lax.broadcasted_iota(jnp.int32, (1, BLK), 1)
    count = jnp.sum(jnp.where(lane == 4 * NB, row, 0.0))
    gram_ref[...] = own_ref[...] / count
    scale = jnp.zeros((1, BLK), jnp.float32)
    for k, levels in enumerate(LEVELS):
        scale = jnp.where(lane // NB == k, levels * levels / (OUT * BLK), scale)
    row = row * scale / count
    for t in range(NT):
        o_ref[t] = row


def totals(rows, own):
    vmem = pl.BlockSpec(memory_space=pltpu.VMEM)
    return pl.pallas_call(
        total_kernel,
        out_shape=(
            jax.ShapeDtypeStruct((NB, ROWS, BLK), jnp.float32),
            jax.ShapeDtypeStruct((NT, 1, BLK), jnp.float32),
        ),
        in_specs=[vmem, vmem],
        out_specs=(vmem, vmem),
        compiler_params=params(),
        name="totals",
    )(rows, own)


def spread_kernel(r_ref, o_ref, row_ref):
    n = NT
    for t in range(n):
        row_ref[t : t + 1, :] = r_ref[t]
    lane = lax.broadcasted_iota(jnp.int32, (8, BLK), 1)
    source = lax.broadcasted_iota(jnp.int32, (8, BLK), 0)
    total = [jnp.zeros((1, BLK), jnp.float32)] * 4
    for h in range(n // 8):
        skewed = pltpu.roll(row_ref[h * 8 : (h + 1) * 8, :], 0, 1, stride=NB, stride_axis=0)
        for k in range(4):
            moved = pltpu.roll(skewed, (h * 8 * NB - k * NB) % BLK, 1)
            kept = jnp.where(lane // NB == source + h * 8, moved, 0.0)
            total[k] = total[k] + jnp.sum(kept, axis=0, keepdims=True)
    for k in range(4):
        o_ref[k : k + 1, :] = total[k]


def spread(rows):
    vmem = pl.BlockSpec(memory_space=pltpu.VMEM)
    return pl.pallas_call(
        spread_kernel,
        out_shape=jax.ShapeDtypeStruct((4, BLK), jnp.float32),
        in_specs=[vmem],
        out_specs=vmem,
        scratch_shapes=[pltpu.VMEM((NT, BLK), jnp.float32)],
        compiler_params=params(),
        name="spread",
    )(rows)


CHUNKS = 2


def quant_kernel(bits_ref, x_ref, w_ref, own_ref, left_ref, right_ref, far_ref, o_ref, c_ref, u_ref, slab_ref):
    rows = w_ref.shape[0] // CHUNKS
    x = x_ref[0]

    def slab(p):
        for off, ref in enumerate((own_ref, right_ref, far_ref, left_ref)):
            base = pl.multiple_of(lax.rem(x + off, NX) * (NZ * ROWS), NZ * ROWS)
            chunk = jnp.concatenate([ref[i, p] for i in range(NZ)], axis=0)
            slab_ref[pl.ds(base, NZ * ROWS), :] = chunk
        return slab_ref[...]

    inv_diag = 1.0 / slab(NP - 1)[:, :NB].T
    p = 0
    for j in range(NB):
        first = j * BLK
        width = PANEL - first - BLK
        if width:
            for i in range(width // BLK):
                u = slab(p)
                p += 1
                high = u.astype(jnp.bfloat16)
                low = (u - high.astype(jnp.float32)).astype(jnp.bfloat16)
                cols = slice(i * BLK, (i + 1) * BLK)
                u_ref[0:BLK, cols] = high
                u_ref[BLK : 2 * BLK, cols] = high
                u_ref[2 * BLK : 3 * BLK, cols] = low
        bits = bits_ref[j]
        levels = jnp.where(bits == 2, 2.0, jnp.where(bits == 3, 4.0, jnp.where(bits == 4, 8.0, 128.0)))
        half = levels - 0.5
        for h in range(CHUNKS):
            part = slice(h * rows, (h + 1) * rows)
            if j == 0:
                c = w_ref[part, :BLK].astype(jnp.float32)
            else:
                c = c_ref[part, first : first + BLK]
            step = (jnp.max(jnp.abs(c), axis=1, keepdims=True) + 1e-6) / half
            u = c * (1.0 / step)
            q = step * jnp.clip(u - sine_over_two_pi(u), -levels, levels - 1.0)
            o_ref[part, first : first + BLK] = q.astype(jnp.bfloat16)
            if width:
                e = (c - q) * inv_diag[j : j + 1, :]
                high = e.astype(jnp.bfloat16)
                low = (e - high.astype(jnp.float32)).astype(jnp.bfloat16)
                lhs = jnp.concatenate([high, low, high], axis=1)
                update = jnp.dot(lhs, u_ref[:, :width], preferred_element_type=jnp.float32)
                if j == 0:
                    rest = w_ref[part, BLK:].astype(jnp.float32)
                else:
                    rest = c_ref[part, first + BLK :]
                c_ref[part, first + BLK :] = rest - update


def quantize(bits, x, weight, factor):
    rows = weight.shape[0]
    return pl.pallas_call(
        quant_kernel,
        out_shape=jax.ShapeDtypeStruct((rows, PANEL), jnp.bfloat16),
        in_specs=[
            pl.BlockSpec(memory_space=pltpu.SMEM),
            pl.BlockSpec(memory_space=pltpu.SMEM),
        ]
        + [pl.BlockSpec(memory_space=pltpu.VMEM)] * 5,
        out_specs=pl.BlockSpec(memory_space=pltpu.VMEM),
        scratch_shapes=[
            pltpu.VMEM((rows, PANEL), jnp.float32),
            pltpu.VMEM((3 * BLK, PANEL - BLK), jnp.bfloat16),
            pltpu.VMEM((BLK, BLK), jnp.float32),
        ],
        compiler_params=params(),
        name="quantize",
    )(bits, x, weight, *factor)


def exchange(pieces, axes):
    return lax.all_to_all(pieces, axes, 0, 0, tiled=False)


def shift_x(piece, by):
    return lax.ppermute(piece, "x", [(i, (i + by) % NX) for i in range(NX)])


def near(array):
    return pltpu.with_memory_space_constraint(array, pltpu.VMEM)


def per_device(activations, token_ids, weight, inv_chol, bit_widths):
    dp = ("x", "z")
    tensor = ("y", "c")
    tokens = token_ids.reshape(1, -1)
    x = lax.axis_index("x").reshape(1).astype(jnp.int32)
    first = (lax.axis_index(dp) * ROWS).reshape(1).astype(jnp.int32)
    partial = gram_partial(tokens, activations)
    rows = exchange(partial, "x")
    grams, diagonals = error_grams(weight)
    packed = sum_x(first, near(inv_chol), near(rows))
    over_z = exchange(packed, "z")
    own, copies = sum_z(near(over_z))
    gram = exchange(copies, dp)
    mine, _ = lax.optimization_barrier((over_z, copies))
    mine = mine[:, :NP]
    left = shift_x(mine, 1)
    right = shift_x(mine, -1)
    row = scores(tokens, near(gram), near(grams), diagonals)
    left_late, _ = lax.optimization_barrier((left, row))
    row = exchange(row, dp)
    far = shift_x(left_late, 1)
    rows = gram_rows(first, near(gram), near(own))
    quantized = quantize(bit_widths, x, weight, tuple(map(near, (mine, left, right, far))))
    gram_out, row = totals(near(row), near(rows))
    row = exchange(row, tensor)
    block_errors = spread(near(row))
    return quantized, gram_out, block_errors.T


def solution(mesh):
    fine = Mesh(mesh.devices.reshape(NX, NZ, NY, NC), ("x", "z", "y", "c"))
    dp = ("x", "z")
    tensor = ("y", "c")
    placed = (P(dp, tensor), P(dp), P(dp, tensor), P(tensor, dp, None), P(tensor))
    return jax.shard_map(
        per_device,
        mesh=fine,
        in_specs=placed,
        out_specs=(P(dp, tensor), P(tensor, dp, None), P()),
        check_vma=False,
    )
```

```python
import jax
import jax.numpy as jnp
from jax import lax
from jax.experimental import pallas as pl
from jax.experimental.pallas import tpu as pltpu
from jax.sharding import Mesh, PartitionSpec as P

OUT = 16384
BLK = 128
PANEL = 1024
NB = 8
DP = 32
ROWS = BLK // DP
NX, NZ, NY, NC = 4, 8, 8, 2
NT = NY * NC
PAIRS = [(j, c) for j in range(NB) for c in range(j + 1, NB)]
NP = len(PAIRS) + 1
HB = NB // 2
GT = HB + 1
DL = NB
PAD = 128004
LEVELS = (2.0, 4.0, 8.0, 128.0)

SIN = (
    0.9999996039231652,
    -6.579691570100355,
    12.986436001995736,
    -12.188101551479916,
    6.558042314696102,
    -1.9530321174789678,
)


def sine_over_two_pi(u):
    r = u - jnp.round(u)
    z = r * r
    p = SIN[-1] * z + SIN[-2]
    for a in SIN[-3::-1]:
        p = p * z + a
    return p * r


def params(*semantics):
    return pltpu.CompilerParams(dimension_semantics=semantics, vmem_limit_bytes=56 << 20)


def gram_kernel(tok_ref, a_ref, o_ref):
    live = jnp.where(tok_ref[...] != PAD, 1.0, 0.0).astype(jnp.bfloat16)
    row = lax.broadcasted_iota(jnp.int32, (BLK, BLK), 0)
    col = lax.broadcasted_iota(jnp.int32, (BLK, BLK), 1)
    diag = jnp.zeros((BLK, BLK), jnp.float32)

    def gram(b):
        x = a_ref[:, b * BLK : (b + 1) * BLK]
        return jnp.dot(x.T * live, x, preferred_element_type=jnp.float32)

    def put(g, tile):
        for d in range(DP):
            o_ref[d // NZ, d % NZ, tile] = g[d * ROWS : (d + 1) * ROWS]

    for b in range(HB):
        lower = gram(b + HB)
        put(jnp.where(col >= row, gram(b), lower), b)
        value = jnp.sum(jnp.where(col == row, lower, 0.0), axis=1, keepdims=True)
        diag = jnp.where(col == DL + b + HB, value, diag)
    put(diag, HB)


def gram_partial(tokens, activations):
    vmem = pl.BlockSpec(memory_space=pltpu.VMEM)
    return pl.pallas_call(
        gram_kernel,
        out_shape=pltpu.VMEM((NX, NZ, GT, ROWS, BLK), jnp.float32),
        in_specs=[vmem, vmem],
        out_specs=vmem,
        compiler_params=params(),
        name="gram_partial",
    )(tokens, activations)


def sum_x_kernel(first_ref, f_ref, g_ref, o_ref):
    lane = lax.broadcasted_iota(jnp.int32, (ROWS, BLK), 1)
    row = lax.broadcasted_iota(jnp.int32, (ROWS, BLK), 0)
    on_diag = lane == row + first_ref[0]
    diag = jnp.zeros((ROWS, BLK), jnp.float32)
    for j in range(NB):
        tile = f_ref[j, :, j * BLK : (j + 1) * BLK]
        value = jnp.sum(jnp.where(on_diag, tile, 0.0), axis=1, keepdims=True)
        diag = jnp.where(lane == j, value, diag)
    for p, (j, c) in enumerate(PAIRS):
        tile = f_ref[j, :, c * BLK : (c + 1) * BLK]
        for i in range(NZ):
            o_ref[i, p] = tile
    for i in range(NZ):
        total = g_ref[0, i]
        for x in range(1, NX):
            total = total + g_ref[x, i]
        o_ref[i, NP:] = total[:HB]
        o_ref[i, NP - 1] = diag + total[HB]


def sum_x(first, factor, received):
    vmem = pl.BlockSpec(memory_space=pltpu.VMEM)
    return pl.pallas_call(
        sum_x_kernel,
        out_shape=jax.ShapeDtypeStruct((NZ, NP + HB, ROWS, BLK), jnp.float32),
        in_specs=[pl.BlockSpec(memory_space=pltpu.SMEM), vmem, vmem],
        out_specs=vmem,
        compiler_params=params(),
        name="sum_x",
    )(first, factor, received)


def sum_z_kernel(g_ref, own_ref, o_ref):
    total = g_ref[0, NP - 1 :]
    for i in range(1, NZ):
        total = total + g_ref[i, NP - 1 :]
    lane = lax.broadcasted_iota(jnp.int32, (ROWS, BLK), 1)
    diag = jnp.where(lane >= DL, total[0], 0.0)
    own_ref[:HB] = total[1:]
    own_ref[HB] = diag
    for d in range(DP):
        o_ref[d, :HB] = total[1:]
        o_ref[d, HB] = diag


def sum_z(received):
    vmem = pl.BlockSpec(memory_space=pltpu.VMEM)
    return pl.pallas_call(
        sum_z_kernel,
        out_shape=(
            pltpu.VMEM((GT, ROWS, BLK), jnp.float32),
            jax.ShapeDtypeStruct((DP, GT, ROWS, BLK), jnp.float32),
        ),
        in_specs=[vmem],
        out_specs=(vmem, vmem),
        compiler_params=params(),
        name="sum_z",
    )(received)


def error_kernel(w_ref, o_ref, d_ref):
    b = pl.program_id(0)
    row = lax.broadcasted_iota(jnp.int32, (BLK, BLK), 0)
    col = lax.broadcasted_iota(jnp.int32, (BLK, BLK), 1)
    upper = jnp.where(col > row, 2.0, jnp.where(col == row, 1.0, 0.0))
    lower = jnp.where(col < row, 2.0, 0.0)
    weight = jnp.where(b < HB, upper, lower)
    w = w_ref[...].astype(jnp.float32)
    bound = jnp.max(jnp.abs(w), axis=1, keepdims=True) + 1e-6
    unit = w * (1.0 / bound)
    for k, levels in enumerate(LEVELS):
        u = unit * (levels - 0.5)
        smooth = jnp.clip(u - sine_over_two_pi(u), -levels, levels - 1.0)
        e = (w - (bound * (1.0 / (levels - 0.5))) * smooth).astype(jnp.bfloat16)
        s = lax.dot_general(e, e, (((0,), (0,)), ((), ())), preferred_element_type=jnp.float32)
        value = jnp.sum(jnp.where(col == row, s, 0.0), axis=1, keepdims=True)
        diag = jnp.where((col == DL + b) & (b >= HB), value, 0.0)
        s = s * weight
        for d in range(DP):
            part = slice(d * ROWS, (d + 1) * ROWS)
            o_ref[0, k, d] = s[part]
            before = jnp.where(b == 0, 0.0, d_ref[k, d])
            d_ref[k, d] = before + diag[part]


def error_grams(weight):
    rows = weight.shape[0]
    return pl.pallas_call(
        error_kernel,
        out_shape=(
            jax.ShapeDtypeStruct((NB, 4, DP, ROWS, BLK), jnp.float32),
            jax.ShapeDtypeStruct((4, DP, ROWS, BLK), jnp.float32),
        ),
        grid=(NB,),
        in_specs=[pl.BlockSpec((rows, BLK), lambda b: (0, b))],
        out_specs=(
            pl.BlockSpec((1, 4, DP, ROWS, BLK), lambda b: (b, 0, 0, 0, 0)),
            pl.BlockSpec((4, DP, ROWS, BLK), lambda b: (0, 0, 0, 0)),
        ),
        compiler_params=params("arbitrary"),
        name="error_grams",
    )(weight)


def score_kernel(tok_ref, g_ref, s_ref, d_ref, o_ref, row_ref):
    row_ref[...] = jnp.zeros((BLK, BLK), jnp.float32)
    live = jnp.where(tok_ref[...] != PAD, 1.0, 0.0)
    row_ref[4 * NB : 4 * NB + 1, :] = sum(live[:, i : i + BLK] for i in range(0, live.shape[1], BLK))
    diagonals = jnp.zeros((1, BLK), jnp.float32)
    for k in range(4):
        for b in range(NB):
            acc = g_ref[0, b % HB] * s_ref[b, k, 0]
            for d in range(1, DP):
                acc = acc + g_ref[d, b % HB] * s_ref[b, k, d]
            row_ref[k * NB + b : k * NB + b + 1, :] = jnp.sum(acc, axis=0, keepdims=True)
        acc = g_ref[0, HB] * d_ref[k, 0]
        for d in range(1, DP):
            acc = acc + g_ref[d, HB] * d_ref[k, d]
        acc = jnp.sum(acc, axis=0, keepdims=True)
        diagonals = diagonals + (acc if k * NB == DL else pltpu.roll(acc, (k * NB - DL) % BLK, 1))
    row = jnp.sum(row_ref[...].T, axis=0, keepdims=True) + diagonals
    for d in range(DP):
        o_ref[d] = row


def scores(tokens, gram, grams, diagonals):
    vmem = pl.BlockSpec(memory_space=pltpu.VMEM)
    return pl.pallas_call(
        score_kernel,
        out_shape=jax.ShapeDtypeStruct((DP, 1, BLK), jnp.float32),
        in_specs=[vmem] * 4,
        out_specs=vmem,
        scratch_shapes=[pltpu.VMEM((BLK, BLK), jnp.float32)],
        compiler_params=params(),
        name="scores",
    )(tokens, gram, grams, diagonals)


def rows_kernel(first_ref, g_ref, own_ref, o_ref):
    first = first_ref[0]
    lane = lax.broadcasted_iota(jnp.int32, (ROWS, BLK), 1)
    mine = lax.broadcasted_iota(jnp.int32, (ROWS, BLK), 0) + first
    pick = jnp.where(
        lax.broadcasted_iota(jnp.int32, (8, BLK), 1) == lax.broadcasted_iota(jnp.int32, (8, BLK), 0) + first, 1.0, 0.0
    )
    for b in range(HB):
        square = jnp.concatenate([g_ref[d, b] for d in range(DP)], axis=0)
        turned = lax.dot_general(
            pick,
            square,
            (((1,), (1,)), ((), ())),
            precision=lax.Precision.HIGHEST,
            preferred_element_type=jnp.float32,
        )[:ROWS]
        own = own_ref[b]
        diag = jnp.sum(jnp.where(lane == DL + b + HB, own_ref[HB], 0.0), axis=1, keepdims=True)
        o_ref[b] = jnp.where(lane >= mine, own, turned)
        o_ref[b + HB] = jnp.where(lane < mine, own, jnp.where(lane == mine, diag, turned))


def gram_rows(first, gram, own):
    vmem = pl.BlockSpec(memory_space=pltpu.VMEM)
    return pl.pallas_call(
        rows_kernel,
        out_shape=pltpu.VMEM((NB, ROWS, BLK), jnp.float32),
        in_specs=[pl.BlockSpec(memory_space=pltpu.SMEM), vmem, vmem],
        out_specs=vmem,
        compiler_params=params(),
        name="gram_rows",
    )(first, gram, own)


def total_kernel(r_ref, own_ref, gram_ref, o_ref):
    row = r_ref[0]
    for d in range(1, DP):
        row = row + r_ref[d]
    lane = lax.broadcasted_iota(jnp.int32, (1, BLK), 1)
    count = jnp.sum(jnp.where(lane == 4 * NB, row, 0.0))
    gram_ref[...] = own_ref[...] / count
    scale = jnp.zeros((1, BLK), jnp.float32)
    for k, levels in enumerate(LEVELS):
        scale = jnp.where(lane // NB == k, levels * levels / (OUT * BLK), scale)
    row = row * scale / count
    for t in range(NT):
        o_ref[t] = row


def totals(rows, own):
    vmem = pl.BlockSpec(memory_space=pltpu.VMEM)
    return pl.pallas_call(
        total_kernel,
        out_shape=(
            jax.ShapeDtypeStruct((NB, ROWS, BLK), jnp.float32),
            jax.ShapeDtypeStruct((NT, 1, BLK), jnp.float32),
        ),
        in_specs=[vmem, vmem],
        out_specs=(vmem, vmem),
        compiler_params=params(),
        name="totals",
    )(rows, own)


def spread_kernel(r_ref, o_ref, row_ref):
    n = NT
    for t in range(n):
        row_ref[t : t + 1, :] = r_ref[t]
    lane = lax.broadcasted_iota(jnp.int32, (8, BLK), 1)
    source = lax.broadcasted_iota(jnp.int32, (8, BLK), 0)
    total = [jnp.zeros((1, BLK), jnp.float32)] * 4
    for h in range(n // 8):
        skewed = pltpu.roll(row_ref[h * 8 : (h + 1) * 8, :], 0, 1, stride=NB, stride_axis=0)
        for k in range(4):
            moved = pltpu.roll(skewed, (h * 8 * NB - k * NB) % BLK, 1)
            kept = jnp.where(lane // NB == source + h * 8, moved, 0.0)
            total[k] = total[k] + jnp.sum(kept, axis=0, keepdims=True)
    for k in range(4):
        o_ref[k : k + 1, :] = total[k]


def spread(rows):
    vmem = pl.BlockSpec(memory_space=pltpu.VMEM)
    return pl.pallas_call(
        spread_kernel,
        out_shape=jax.ShapeDtypeStruct((4, BLK), jnp.float32),
        in_specs=[vmem],
        out_specs=vmem,
        scratch_shapes=[pltpu.VMEM((NT, BLK), jnp.float32)],
        compiler_params=params(),
        name="spread",
    )(rows)


CHUNKS = 2


def quant_kernel(bits_ref, x_ref, w_ref, own_ref, left_ref, right_ref, far_ref, o_ref, c_ref, u_ref, slab_ref):
    rows = w_ref.shape[0] // CHUNKS
    x = x_ref[0]

    def slab(p):
        for off, ref in enumerate((own_ref, right_ref, far_ref, left_ref)):
            base = pl.multiple_of(lax.rem(x + off, NX) * (NZ * ROWS), NZ * ROWS)
            chunk = jnp.concatenate([ref[i, p] for i in range(NZ)], axis=0)
            slab_ref[pl.ds(base, NZ * ROWS), :] = chunk
        return slab_ref[...]

    inv_diag = 1.0 / slab(NP - 1)[:, :NB].T
    p = 0
    for j in range(NB):
        first = j * BLK
        width = PANEL - first - BLK
        if width:
            for i in range(width // BLK):
                u = slab(p)
                p += 1
                high = u.astype(jnp.bfloat16)
                low = (u - high.astype(jnp.float32)).astype(jnp.bfloat16)
                cols = slice(i * BLK, (i + 1) * BLK)
                u_ref[0:BLK, cols] = high
                u_ref[BLK : 2 * BLK, cols] = high
                u_ref[2 * BLK : 3 * BLK, cols] = low
        bits = bits_ref[j]
        levels = jnp.where(bits == 2, 2.0, jnp.where(bits == 3, 4.0, jnp.where(bits == 4, 8.0, 128.0)))
        half = levels - 0.5
        for h in range(CHUNKS):
            part = slice(h * rows, (h + 1) * rows)
            if j == 0:
                c = w_ref[part, :BLK].astype(jnp.float32)
            else:
                c = c_ref[part, first : first + BLK]
            step = (jnp.max(jnp.abs(c), axis=1, keepdims=True) + 1e-6) / half
            u = c * (1.0 / step)
            q = step * jnp.clip(u - sine_over_two_pi(u), -levels, levels - 1.0)
            o_ref[part, first : first + BLK] = q.astype(jnp.bfloat16)
            if width:
                e = (c - q) * inv_diag[j : j + 1, :]
                high = e.astype(jnp.bfloat16)
                low = (e - high.astype(jnp.float32)).astype(jnp.bfloat16)
                lhs = jnp.concatenate([high, low, high], axis=1)
                update = jnp.dot(lhs, u_ref[:, :width], preferred_element_type=jnp.float32)
                if j == 0:
                    rest = w_ref[part, BLK:].astype(jnp.float32)
                else:
                    rest = c_ref[part, first + BLK :]
                c_ref[part, first + BLK :] = rest - update


def quantize(bits, x, weight, factor):
    rows = weight.shape[0]
    return pl.pallas_call(
        quant_kernel,
        out_shape=jax.ShapeDtypeStruct((rows, PANEL), jnp.bfloat16),
        in_specs=[
            pl.BlockSpec(memory_space=pltpu.SMEM),
            pl.BlockSpec(memory_space=pltpu.SMEM),
        ]
        + [pl.BlockSpec(memory_space=pltpu.VMEM)] * 5,
        out_specs=pl.BlockSpec(memory_space=pltpu.VMEM),
        scratch_shapes=[
            pltpu.VMEM((rows, PANEL), jnp.float32),
            pltpu.VMEM((3 * BLK, PANEL - BLK), jnp.bfloat16),
            pltpu.VMEM((BLK, BLK), jnp.float32),
        ],
        compiler_params=params(),
        name="quantize",
    )(bits, x, weight, *factor)


def exchange(pieces, axes):
    return lax.all_to_all(pieces, axes, 0, 0, tiled=False)


def shift_x(piece, by):
    return lax.ppermute(piece, "x", [(i, (i + by) % NX) for i in range(NX)])


def near(array):
    return pltpu.with_memory_space_constraint(array, pltpu.VMEM)


def per_device(activations, token_ids, weight, inv_chol, bit_widths):
    dp = ("x", "z")
    tensor = ("y", "c")
    tokens = token_ids.reshape(1, -1)
    x = lax.axis_index("x").reshape(1).astype(jnp.int32)
    first = (lax.axis_index(dp) * ROWS).reshape(1).astype(jnp.int32)
    partial = gram_partial(tokens, activations)
    rows = exchange(partial, "x")
    grams, diagonals = error_grams(weight)
    packed = sum_x(first, near(inv_chol), near(rows))
    over_z = exchange(packed, "z")
    own, copies = sum_z(near(over_z))
    gram = exchange(copies, dp)
    mine, _ = lax.optimization_barrier((over_z, copies))
    mine = mine[:, :NP]
    left = shift_x(mine, 1)
    right = shift_x(mine, -1)
    row = scores(tokens, near(gram), near(grams), diagonals)
    left_late, _ = lax.optimization_barrier((left, row))
    row = exchange(row, dp)
    far = shift_x(left_late, 1)
    rows = gram_rows(first, near(gram), near(own))
    quantized = quantize(bit_widths, x, weight, tuple(map(near, (mine, left, right, far))))
    gram_out, row = totals(near(row), near(rows))
    row = exchange(row, tensor)
    block_errors = spread(near(row))
    return quantized, gram_out, block_errors.T


def solution(mesh):
    fine = Mesh(mesh.devices.reshape(NX, NZ, NY, NC), ("x", "z", "y", "c"))
    dp = ("x", "z")
    tensor = ("y", "c")
    placed = (P(dp, tensor), P(dp), P(dp, tensor), P(tensor, dp, None), P(tensor))
    return jax.shard_map(
        per_device,
        mesh=fine,
        in_specs=placed,
        out_specs=(P(dp, tensor), P(tensor, dp, None), P()),
        check_vma=False,
    )
```
